128 devices in a mesh: dp: 64 (over z_lo, x, y, core), tensor: 2 (over z_hi).
Axes of the slice: x: 4, y: 4, z: 4 (z_hi: 2, z_lo: 2; z = z_hi * 2 + z_lo), core: 2. Of those that a mesh axis runs over, the one named last changes fastest.
Arguments:
- tokens: bfloat16 [16384, 1152], P(('dp', 'tensor')), may hold values from -6 to 6
- segment_ids: int32 [64, 256], P('dp'), may hold values from 0 to 7, never falling along the last dimension, each value on 1 to 192 neighbouring positions
- w_query: bfloat16 [1152, 1024], P('dp', 'tensor'), may hold values from -1 to 1
- w_key: bfloat16 [1152, 256], P('dp'), may hold values from -1 to 1
- w_value: bfloat16 [1152, 256], P('dp'), may hold values from -0.1875 to 0.1875
- w_out: bfloat16 [1152, 1024], P('dp', 'tensor'), may hold values from -0.1875 to 0.1875
- gain_query: bfloat16 [256], P('dp'), may hold values from -1 to 4
- gain_key: bfloat16 [256], P('dp'), may hold values from -1 to 4
- gain_pre_attn: bfloat16 [1152], P('dp'), may hold values from -0.5 to 0.5
- gain_post_attn: bfloat16 [1152], P('dp'), may hold values from -0.5 to 0.5
- w_gate: bfloat16 [1152, 6912], P('dp', 'tensor'), may hold values from -0.1875 to 0.1875
- w_up: bfloat16 [1152, 6912], P('dp', 'tensor'), may hold values from -0.1875 to 0.1875
- w_down: bfloat16 [1152, 6912], P('dp', 'tensor'), may hold values from -0.078125 to 0.078125
- gain_pre_ffn: bfloat16 [1152], P('dp'), may hold values from -0.5 to 0.5
- gain_post_ffn: bfloat16 [1152], P('dp'), may hold values from -0.5 to 0.5
- cotangent: bfloat16 [16384, 1152], P(('dp', 'tensor')), may hold values from -6 to 6
Outputs:
- output: bfloat16 [16384, 1152], P(('dp', 'tensor'))
- grad_tokens: float32 [16384, 1152], P(('dp', 'tensor'))
- grad_w_query: float32 [1152, 1024], P('dp', 'tensor')
- grad_w_key: float32 [1152, 256], P('dp')
- grad_w_value: float32 [1152, 256], P('dp')
- grad_w_out: float32 [1152, 1024], P('dp', 'tensor')
- grad_gain_query: float32 [256], P('dp')
- grad_gain_key: float32 [256], P('dp')
- grad_gain_pre_attn: float32 [1152], P('dp')
- grad_gain_post_attn: float32 [1152], P('dp')
- grad_w_gate: float32 [1152, 6912], P('dp', 'tensor')
- grad_w_up: float32 [1152, 6912], P('dp', 'tensor')
- grad_w_down: float32 [1152, 6912], P('dp', 'tensor')
- grad_gain_pre_ffn: float32 [1152], P('dp')
- grad_gain_post_ffn: float32 [1152], P('dp')
The draws below stay inside these ranges and needn't reach their ends.
Inputs may be any that keep to these rules, and one draw needn't show every extreme that they name: `segment_ids`: in each pack the ids run from 0 to 7 without falling; every sequence has 1 to 192 tokens and one has exactly 192.
All inputs are finite; a program needn't handle non-finite values.
Results may differ from the reference program's by a relative error of at most 0.024.
The reference program's roundings to bfloat16 on the way count: a program that leaves them out, or rounds other values in their place, can miss the bound.
Values may be sent and summed in bfloat16 or wider, within the bound.
A program may use at most 192 MiB of HBM per device.

```python
import math
import jax
import jax.numpy as jnp
import numpy as np
from jax import lax

D = 1152
HEADS = 4
HEAD = 256
FF = 6912
TOK_DEV = 256
SEQ_MAX = 192
SEG_COUNT = 8
SHARDS = 64
TOKENS = 16384
N_TENSOR = 2


def key_matrix(key):
    normal_draw = jax.random.normal(jax.random.fold_in(key, 101), (D, HEAD), jnp.float32)
    return jnp.clip(normal_draw, -4.0, 4.0) * D ** (-0.5)


def draw_w_key(key, part):
    return key_matrix(key).astype(jnp.bfloat16)


def draw_w_query(key, part):
    normal_draw = jax.random.normal(jax.random.fold_in(key, 103), (D, HEADS * HEAD), jnp.float32)
    fresh = jnp.clip(normal_draw, -4.0, 4.0) * D ** (-0.5)
    return fresh.astype(jnp.bfloat16)


def draw_gain_query(key, part):
    return jax.random.uniform(jax.random.fold_in(key, 107), (HEAD,), jnp.float32, -0.3, 0.7).astype(jnp.bfloat16)


def draw_gain_key(key, part):
    return jax.random.uniform(jax.random.fold_in(key, 109), (HEAD,), jnp.float32, -0.3, 0.7).astype(jnp.bfloat16)


def steps_of(key, shape, shards, smallest, largest):
    loudness = 1.0
    for axis_at, blocks in shards:
        heights = jax.random.uniform(jax.random.fold_in(jax.random.fold_in(key, 6), axis_at), (blocks,), jnp.float32, smallest / len(shards), largest / len(shards))
        loudness = loudness * jnp.repeat(jnp.exp(heights), shape[axis_at] // blocks).reshape((-1,) + (1,) * (len(shape) - 1 - axis_at))
    return loudness


def split_up(amount, total, bound, skew):
    loads = [(1 << 20) // math.isqrt(rank ** skew) + 1 for rank in range(2, amount + 1)]
    rest, holding = total - bound - (amount - 1), [1] * (amount - 1)
    while rest > 0:
        candidates = [i for i in range(amount - 1) if holding[i] < bound]
        whole, left = sum([loads[i] for i in candidates]), rest
        for i in candidates:
            extra = min(bound - holding[i], max(1, left * loads[i] // whole), rest)
            holding[i] = holding[i] + extra
            rest = rest - extra
    return np.array([bound] + holding)


def uneven_parts(own_key, amount, total, limit, lean):
    if amount == 2:
        one = jax.random.randint(own_key, (), max(1, total - limit), min(limit, total - 1) + 1)
        return jnp.stack([one, total - one])
    tallies = jnp.asarray(split_up(amount, total, limit, lean), jnp.int32)
    twos = (amount - 1) // 2
    source_of, taker = tallies[1:1 + 2 * twos:2], tallies[2:2 + 2 * twos:2]
    room = jnp.minimum(source_of - 1, limit - taker)
    moved = jax.random.randint(jax.random.fold_in(own_key, 1), (twos,), 0, 1 << 20) % (room + 1)
    tallies = tallies.at[1:1 + 2 * twos:2].set(source_of - moved).at[2:2 + 2 * twos:2].set(taker + moved)
    return tallies[jax.random.permutation(jax.random.fold_in(own_key, 2), amount)]


def gaussian(stream_key, shape, scale, most, split=(), kind=jnp.bfloat16):
    factor_of = steps_of(stream_key, shape, split, -0.22, 0.18) if split else 1.0
    array = jax.random.normal(stream_key, shape, jnp.float32) * scale * factor_of
    return jnp.minimum(jnp.maximum(array, -most), most).astype(kind)


def setup_inputs(seed: int = 0) -> dict:
    keys = jax.random.split(jax.random.key(seed), 17)
    return {
        "tokens": gaussian(keys[0], (TOKENS, D), 1.0, 6.0, ((0, 128),)),
        "segment_ids": jax.vmap(lambda own: jnp.searchsorted(jnp.cumsum(uneven_parts(own, SEG_COUNT, TOK_DEV, SEQ_MAX, 2)), jnp.arange(TOK_DEV), side="right"))(jax.random.split(keys[1], SHARDS)).reshape((SHARDS, TOK_DEV)).astype(jnp.int32),
        "w_query": draw_w_query(jax.random.fold_in(keys[16], 71), 0),
        "w_key": draw_w_key(jax.random.fold_in(keys[16], 71), 0),
        "w_value": gaussian(keys[4], (D, HEAD), D ** -0.5, 0.1875, ((0, 64),)),
        "w_out": gaussian(keys[5], (D, HEADS * HEAD), (HEADS * HEAD) ** -0.5, 0.1875, ((0, 64), (1, 2))),
        "gain_query": draw_gain_query(jax.random.fold_in(keys[16], 71), 0),
        "gain_key": draw_gain_key(jax.random.fold_in(keys[16], 71), 0),
        "gain_pre_attn": jnp.clip(jax.random.uniform(keys[8], (D,), jnp.float32, -0.5, 0.5) * steps_of(keys[8], (D,), ((0, 64),), -0.4, 0.0), -0.5, 0.5).astype(jnp.bfloat16),
        "gain_post_attn": jnp.clip(jax.random.uniform(keys[9], (D,), jnp.float32, -0.5, 0.5) * steps_of(keys[9], (D,), ((0, 64),), -0.4, 0.0), -0.5, 0.5).astype(jnp.bfloat16),
        "w_gate": gaussian(keys[10], (D, FF), D ** -0.5, 0.1875, ((0, 64), (1, 2))),
        "w_up": gaussian(keys[11], (D, FF), D ** -0.5, 0.1875, ((0, 64), (1, 2))),
        "w_down": gaussian(keys[12], (D, FF), FF ** -0.5, 0.078125, ((0, 64), (1, 2))),
        "gain_pre_ffn": jnp.clip(jax.random.uniform(keys[13], (D,), jnp.float32, -0.5, 0.5) * steps_of(keys[13], (D,), ((0, 64),), -0.4, 0.0), -0.5, 0.5).astype(jnp.bfloat16),
        "gain_post_ffn": jnp.clip(jax.random.uniform(keys[14], (D,), jnp.float32, -0.5, 0.5) * steps_of(keys[14], (D,), ((0, 64),), -0.4, 0.0), -0.5, 0.5).astype(jnp.bfloat16),
        "cotangent": gaussian(keys[15], (TOKENS, D), 1.0, 6.0, ((0, 128),)),
    }


eps = 1e-06
gelu_scale = 0.7978845608028654
gelu_cube = 0.044715

def rms_apply(values, gain_vec):
    inverse = lax.rsqrt(lax.optimization_barrier(jnp.mean(values * values, axis=-1, keepdims=True)) + eps)
    return (values * inverse * (1.0 + gain_vec), inverse)

def rms_back(values, inverse, gain_vec, grad_out):
    scaled = grad_out * (1.0 + gain_vec)
    grad_value = inverse * scaled - values * inverse * inverse * inverse * lax.optimization_barrier(jnp.mean(scaled * values, axis=-1, keepdims=True))
    grad_gain = lax.optimization_barrier(jnp.sum(grad_out * values * inverse, axis=tuple(range(values.ndim - 1))))
    return (grad_value, grad_gain)

def gelu_pair(values):
    tanh_value = jnp.tanh(gelu_scale * (values + gelu_cube * values * values * values))
    result = 0.5 * values * (1.0 + tanh_value)
    slope = 0.5 * (1.0 + tanh_value) + 0.5 * values * (1.0 - tanh_value * tanh_value) * gelu_scale * (1.0 + 3.0 * gelu_cube * values * values)
    return (result, slope)

def positions_of(segment_row):
    token_index = jnp.arange(segment_row.shape[0], dtype=jnp.int32)
    earlier = jnp.concatenate([segment_row[:1] - 1, segment_row[:-1]])
    starts = lax.cummax(jnp.where(segment_row != earlier, token_index, 0), axis=0)
    return token_index - starts

def build_allowed(segment_row):
    token_index = jnp.arange(segment_row.shape[0], dtype=jnp.int32)
    same_seq = segment_row[:, None] == segment_row[None, :]
    causal = token_index[None, :] <= token_index[:, None]
    return same_seq & causal

def rope_tables(position, width):
    half_width = width // 2
    frequency = jnp.exp(jnp.arange(half_width, dtype=jnp.float32) * (-2.0 * math.log(10000.0) / width))
    angles = position.astype(jnp.float32)[:, None] * frequency[None, :]
    cosine_table = jnp.concatenate([jnp.cos(angles), jnp.cos(angles)], axis=1)
    sine_table = jnp.concatenate([jnp.sin(angles), jnp.sin(angles)], axis=1)
    return (cosine_table, sine_table)

def rotate_half(values):
    half_width = values.shape[-1] // 2
    return jnp.concatenate([-values[..., half_width:], values[..., :half_width]], axis=-1)

def shard_pass(weights, token_block, segment_row, cot_block):
    query_mat, key_mat, value_mat, out_mat, gain_q, gain_k, gain_pa, gain_po, gate_mat, up_mat, down_mat, gain_pf, gain_pp = weights
    f32 = jnp.float32
    bf16 = jnp.bfloat16
    resid_in = token_block.astype(f32)
    row_count = resid_in.shape[0]
    attn_in, r_one = rms_apply(resid_in, gain_pa)
    attn_in = attn_in.astype(bf16)
    position = positions_of(segment_row)
    allowed = build_allowed(segment_row)
    query_raw = jnp.dot(attn_in, query_mat, preferred_element_type=f32).reshape(row_count, HEADS, HEAD)
    key_raw = jnp.dot(attn_in, key_mat, preferred_element_type=f32)
    value_vec = jnp.dot(attn_in, value_mat, preferred_element_type=f32).astype(bf16)
    query_norm, r_query = rms_apply(query_raw, gain_q)
    key_norm, r_key = rms_apply(key_raw, gain_k)
    cosine_table, sine_table = rope_tables(position, HEAD)
    query_rot = (query_norm * cosine_table[:, None, :] + rotate_half(query_norm) * sine_table[:, None, :]).astype(bf16)
    key_rot = (key_norm * cosine_table + rotate_half(key_norm) * sine_table).astype(bf16)
    score_scale = HEAD ** (-0.5)
    scores = jnp.einsum('qhd,kd->hqk', query_rot.astype(f32), key_rot.astype(f32)) * score_scale
    scores = jnp.where(allowed[None], scores, -jnp.inf)
    row_max = lax.optimization_barrier(jnp.max(scores, axis=-1, keepdims=True))
    row_total = lax.optimization_barrier(jnp.sum(jnp.exp(scores - row_max), axis=-1, keepdims=True))
    log_total = row_max + jnp.log(row_total)
    weights_full = jnp.where(allowed[None], jnp.exp(scores - log_total), 0.0)
    probs = weights_full.astype(bf16)
    context = jnp.einsum('hqk,kd->qhd', probs.astype(f32), value_vec.astype(f32)).astype(bf16).reshape(row_count, HEADS * HEAD)
    attn_raw = jnp.dot(context, out_mat.T, preferred_element_type=f32)
    attn_normed, r_two = rms_apply(attn_raw, gain_po)
    residual = resid_in + attn_normed
    ffn_input, r_three = rms_apply(residual, gain_pf)
    ffn_input = ffn_input.astype(bf16)
    gate_pre = jnp.dot(ffn_input, gate_mat, preferred_element_type=f32)
    up_proj = jnp.dot(ffn_input, up_mat, preferred_element_type=f32)
    gate_act, gate_slope = gelu_pair(gate_pre)
    hidden_act = (gate_act * up_proj).astype(bf16)
    ffn_raw = jnp.dot(hidden_act, down_mat.T, preferred_element_type=f32)
    ffn_normed, r_four = rms_apply(ffn_raw, gain_pp)
    block_out = (residual + ffn_normed).astype(bf16)
    grad_out = cot_block.astype(f32)
    d_ffn_raw, grad_gpp = rms_back(ffn_raw, r_four, gain_pp, grad_out)
    d_ffn_raw = d_ffn_raw.astype(bf16)
    d_hidden = jnp.dot(d_ffn_raw, down_mat, preferred_element_type=f32)
    grad_down = jnp.dot(d_ffn_raw.T, hidden_act, preferred_element_type=f32)
    d_gate = (d_hidden * up_proj * gate_slope).astype(bf16)
    d_up = (d_hidden * gate_act).astype(bf16)
    d_ffn_input = jnp.dot(d_gate, gate_mat.T, preferred_element_type=f32) + jnp.dot(d_up, up_mat.T, preferred_element_type=f32)
    grad_gate = jnp.dot(ffn_input.T, d_gate, preferred_element_type=f32)
    grad_up = jnp.dot(ffn_input.T, d_up, preferred_element_type=f32)
    d_resid_norm, grad_gpf = rms_back(residual, r_three, gain_pf, d_ffn_input)
    d_residual = grad_out + d_resid_norm
    d_attn_raw, grad_gpo = rms_back(attn_raw, r_two, gain_po, d_residual)
    d_attn_raw = d_attn_raw.astype(bf16)
    d_context = jnp.dot(d_attn_raw, out_mat, preferred_element_type=f32).astype(bf16).reshape(row_count, HEADS, HEAD)
    grad_out_mat = jnp.dot(d_attn_raw.T, context, preferred_element_type=f32)
    d_prob = jnp.einsum('qhd,kd->hqk', d_context.astype(f32), value_vec.astype(f32))
    delta = lax.optimization_barrier(jnp.sum(weights_full * d_prob, axis=-1, keepdims=True))
    d_score = (weights_full * (d_prob - delta) * score_scale).astype(bf16)
    d_query_rot = jnp.einsum('hqk,kd->qhd', d_score.astype(f32), key_rot.astype(f32))
    d_query_norm = d_query_rot * cosine_table[:, None, :] - rotate_half(d_query_rot * sine_table[:, None, :])
    d_query, grad_gq = rms_back(query_raw, r_query, gain_q, d_query_norm)
    d_query = d_query.astype(bf16).reshape(row_count, HEADS * HEAD)
    d_attn_in = jnp.dot(d_query, query_mat.T, preferred_element_type=f32)
    grad_query = jnp.dot(attn_in.T, d_query, preferred_element_type=f32)
    grad_key = jnp.zeros((D, HEAD), f32)
    grad_value = jnp.zeros((D, HEAD), f32)
    grad_gk = jnp.zeros((HEAD,), f32)
    group_size = HEADS // N_TENSOR
    for group_index in range(N_TENSOR):
        first_head = group_index * group_size
        last_head = first_head + group_size
        d_key_rot = jnp.einsum('hqk,qhd->kd', d_score[first_head:last_head].astype(f32), query_rot[:, first_head:last_head].astype(f32))
        d_key_norm = d_key_rot * cosine_table - rotate_half(d_key_rot * sine_table)
        d_key, grad_gk_part = rms_back(key_raw, r_key, gain_k, d_key_norm)
        d_key = d_key.astype(bf16)
        d_value = jnp.einsum('hqk,qhd->kd', probs[first_head:last_head].astype(f32), d_context[:, first_head:last_head].astype(f32)).astype(bf16)
        d_attn_in = d_attn_in + jnp.dot(d_key, key_mat.T, preferred_element_type=f32) + jnp.dot(d_value, value_mat.T, preferred_element_type=f32)
        grad_key = grad_key + jnp.dot(attn_in.T, d_key, preferred_element_type=f32)
        grad_value = grad_value + jnp.dot(attn_in.T, d_value, preferred_element_type=f32)
        grad_gk = grad_gk + grad_gk_part
    d_input_norm, grad_gpa = rms_back(resid_in, r_one, gain_pa, d_attn_in)
    grad_input = d_residual + d_input_norm
    grads = (grad_query, grad_key, grad_value, grad_out_mat, grad_gq, grad_gk, grad_gpa, grad_gpo, grad_gate, grad_up, grad_down, grad_gpf, grad_gpp)
    return (block_out, grad_input, grads)

def reference(tokens, segment_ids, w_query, w_key, w_value, w_out, gain_query, gain_key, gain_pre_attn, gain_post_attn, w_gate, w_up, w_down, gain_pre_ffn, gain_post_ffn, cotangent):
    f32 = jnp.float32
    weights = (w_query, w_key, w_value, w_out, gain_query.astype(f32), gain_key.astype(f32), gain_pre_attn.astype(f32), gain_post_attn.astype(f32), w_gate, w_up, w_down, gain_pre_ffn.astype(f32), gain_post_ffn.astype(f32))
    zero_grads = (jnp.zeros((D, HEADS * HEAD), f32), jnp.zeros((D, HEAD), f32), jnp.zeros((D, HEAD), f32), jnp.zeros((D, HEADS * HEAD), f32), jnp.zeros((HEAD,), f32), jnp.zeros((HEAD,), f32), jnp.zeros((D,), f32), jnp.zeros((D,), f32), jnp.zeros((D, FF), f32), jnp.zeros((D, FF), f32), jnp.zeros((D, FF), f32), jnp.zeros((D,), f32), jnp.zeros((D,), f32))

    def shard_step(running, inputs):
        token_block, segment_row, cot_block = inputs
        block_out, grad_input, grads = shard_pass(weights, token_block, segment_row, cot_block)
        return (tuple((left + right for left, right in zip(running, grads))), (block_out, grad_input))
    token_blocks = tokens.reshape(SHARDS, TOK_DEV, D)
    cot_blocks = cotangent.reshape(SHARDS, TOK_DEV, D)
    totals, (out_blocks, grad_blocks) = lax.scan(shard_step, zero_grads, (token_blocks, segment_ids, cot_blocks))
    return (out_blocks.reshape(TOKENS, D), grad_blocks.reshape(TOKENS, D), totals[0], totals[1], totals[2], totals[3], totals[4], totals[5], totals[6], totals[7], totals[8], totals[9], totals[10], totals[11], totals[12])
```

```python
import functools
import math

import jax
import jax.numpy as jnp
from jax import lax
from jax.experimental import pallas as pl
from jax.experimental.pallas import tpu as pltpu
from jax.sharding import PartitionSpec as P

eps = 1e-06
gelu_scale = 0.7978845608028654
gelu_cube = 0.044715


def rms_apply(values, gain_vec):
    inverse = lax.rsqrt(jnp.mean(values * values, axis=-1, keepdims=True) + eps)
    return (values * inverse * (1.0 + gain_vec), inverse)


def rms_back(values, inverse, gain_vec, grad_out):
    scaled = grad_out * (1.0 + gain_vec)
    grad_value = inverse * scaled - values * inverse * inverse * inverse * jnp.mean(
        scaled * values, axis=-1, keepdims=True
    )
    grad_gain = jnp.sum(grad_out * values * inverse, axis=tuple(range(values.ndim - 1)))
    return (grad_value, grad_gain)


def positions_of(segment_row):
    token_index = jnp.arange(segment_row.shape[0], dtype=jnp.int32)
    earlier = jnp.concatenate([segment_row[:1] - 1, segment_row[:-1]])
    starts = lax.cummax(jnp.where(segment_row != earlier, token_index, 0), axis=0)
    return token_index - starts


def build_allowed(segment_row):
    token_index = jnp.arange(segment_row.shape[0], dtype=jnp.int32)
    same_seq = segment_row[:, None] == segment_row[None, :]
    causal = token_index[None, :] <= token_index[:, None]
    return same_seq & causal


def rope_tables(position, width):
    half_width = width // 2
    frequency = jnp.exp(
        jnp.arange(half_width, dtype=jnp.float32) * (-2.0 * math.log(10000.0) / width)
    )
    angles = position.astype(jnp.float32)[:, None] * frequency[None, :]
    cosine_table = jnp.concatenate([jnp.cos(angles), jnp.cos(angles)], axis=1)
    sine_table = jnp.concatenate([jnp.sin(angles), jnp.sin(angles)], axis=1)
    return (cosine_table, sine_table)


def rotate_half(values):
    half_width = values.shape[-1] // 2
    return jnp.concatenate([-values[..., half_width:], values[..., :half_width]], axis=-1)


f32 = jnp.float32
bf16 = jnp.bfloat16
MESH = pl.DeviceIdType.MESH
ROWS = 144
SHARD = 18
VMEM_SPEC = pl.BlockSpec(memory_space=pltpu.VMEM)
ANY_SPEC = pl.BlockSpec(memory_space=pl.ANY)
VMEM_MOST = 66_000_000

CLASSES = (
    (0, 2, "zxy"),
    (2, 4, "zyx"),
    (4, 6, "xyz"),
    (6, 8, "yxz"),
    (8, 10, "zxy"),
    (10, 12, "zyx"),
)


def coords():
    dp, t = lax.axis_index("dp"), lax.axis_index("tensor")
    return {"c": lax.rem(dp, 2), "y": lax.rem(dp // 2, 4), "x": lax.rem(dp // 8, 4), "z": dp // 32, "t": t}


def device(at, **change):
    p = {**at, **change}
    return (((p["z"] * 4 + p["x"]) * 4 + p["y"]) * 2 + p["c"], p["t"])


def ahead(at, dim, by):
    size = 2 if dim == "z" else 4
    return lax.rem(at[dim] + by + size, size)


def block_sources():
    attn = [("q", j) for j in range(4)] + [("k", j) for j in range(2)]
    attn_two = [("v", j) for j in range(2)] + [("o", j) for j in range(4)]
    ffn = [[(n, j) for n in "gud" for j in range(14)], [(n, j + 14) if j < 13 else None for n in "gud" for j in range(14)]]
    return [attn + ffn[0], attn_two + ffn[1]]


def enter(peers):
    barrier = pltpu.get_barrier_semaphore()
    for peer in peers:
        pl.semaphore_signal(barrier, inc=1, device_id=peer, device_id_type=MESH)
    pl.semaphore_wait(barrier, len(peers))


def remote(src, dst, send, recv, to):
    return pltpu.make_async_remote_copy(
        src_ref=src, dst_ref=dst, send_sem=send, recv_sem=recv, device_id=to, device_id_type=MESH
    )


def group_peers(at):
    peers = []
    for dy in range(4):
        for dc in range(2):
            if dy or dc:
                peers.append({**at, "y": ahead(at, "y", dy), "c": lax.rem(at["c"] + dc, 2)})
    return peers


def slot_of(p):
    return p["c"] * 4 + p["y"]


def part_of(buf, at, done, dim, index, i0, i1):
    pick = {d: (slice(None) if d in done else at[d]) for d in "zxy"}
    if dim is not None:
        pick[dim] = index
    return buf.at[pick["y"], i0:i1, pick["z"], pick["x"]]


def size_of(done, n):
    size = n * ROWS * 128 * 2
    for d in done:
        size *= 2 if d == "z" else 4
    return size


def order_gather(classes, rate=46e3, hop=1.6):
    free, events, queue = {}, [], []
    for k, (i0, i1, order) in enumerate(classes):
        queue.append((0.0, k, 0, 0))
    while queue:
        queue.sort()
        ready, k, ph, st = queue.pop(0)
        i0, i1, order = classes[k]
        events.append((k, ph, st))
        if ph == len(order):
            continue
        dim, done = order[ph], order[:ph]
        size = size_of(done, i1 - i0)
        if dim == "z":
            ways, moved, follow = ("z+",), size, (k, ph + 1, 0)
        elif st == 0:
            ways, moved, follow = (dim + "+", dim + "-"), size, (k, ph, 1)
        else:
            ways, moved, follow = (dim + "+", dim + "-"), size / 2, (k, ph + 1, 0)
        end = 0.0
        for way in ways:
            free[way] = max(ready, free.get(way, 0.0)) + moved / rate
            end = max(end, free[way])
        queue.append((end + hop, *follow))
    return events


def gather_kernel(
    q_ref, k_ref, v_ref, o_ref, g_ref, u_ref, d_ref, gains_ref, tok_ref,
    buf, other, gbuf, tok_out,
    send, got, own32, own, ggot, gmine,
    a_send, a_recv, g_send, g_recv, s_sem, r_sem, e_sem, l_sem,
):
    at = coords()
    refs = {"q": q_ref, "k": k_ref, "v": v_ref, "o": o_ref, "g": g_ref, "u": u_ref, "d": d_ref}
    group = group_peers(at)
    partner = device(at, c=1 - at["c"])
    mirror = device(at, t=1 - at["t"])
    ring = [device(at, x=ahead(at, "x", 1)), device(at, x=ahead(at, "x", -1)), device(at, z=1 - at["z"])]
    for k, blocks in enumerate(block_sources()):
        for pos, source in enumerate(blocks):
            y, i = divmod(pos, 12)
            if source is None:
                send[k * 4 + y, i] = jnp.zeros((SHARD, 128), bf16)
            else:
                name, j = source
                send[k * 4 + y, i] = refs[name][:, j * 128 : (j + 1) * 128]
    row = lax.broadcasted_iota(jnp.int32, (8, 128), 0)
    gmine[...] = jnp.where(row == at["y"] * 2 + at["c"], gains_ref[...], 0.0)
    me = slot_of(at)
    mine = at["y"] * 2 + at["c"]
    enter([device(p) for p in group] + ring + [mirror])
    tok = remote(tok_ref, tok_out.at[at["t"]], e_sem.at[2], e_sem.at[3], mirror)
    tok.start()
    tok_local = pltpu.make_async_copy(tok_ref, tok_out.at[at["t"]], l_sem.at[1])
    tok_local.start()
    first = []
    for n, p in enumerate(group):
        copy = remote(send.at[slot_of(p)], got.at[mine], a_send.at[n], a_recv.at[mine], device(p))
        small = remote(gmine, ggot.at[mine], g_send.at[n], g_recv.at[mine], device(p))
        copy.start()
        small.start()
        first += [copy, small]
    here = pltpu.make_async_copy(send.at[me], got.at[mine], l_sem.at[0])
    here.start()
    here.wait()
    for p in group:
        s = p["y"] * 2 + p["c"]
        remote(send.at[0], got.at[s], a_send.at[0], a_recv.at[s], device(p)).wait_recv()
        remote(gmine, ggot.at[s], g_send.at[0], g_recv.at[s], device(p)).wait_recv()
    ggot[mine] = gmine[...]
    gmine_sum = ggot[0]
    for s in range(1, 8):
        gmine_sum = gmine_sum + ggot[s]

    @pl.loop(0, 12)
    def _(i):
        for s in range(8):
            own32[SHARD * s : SHARD * (s + 1), :] = got[s, i].astype(f32)
        own[i] = own32[...].astype(bf16)

    for copy in first:
        copy.wait_send()
    gmine[...] = gmine_sum
    local = pltpu.make_async_copy(own, part_of(buf, at, "", None, None, 0, 12), l_sem.at[0])
    local.start()
    glocal = pltpu.make_async_copy(gmine, gbuf.at[at["z"], at["x"]], l_sem.at[2])
    glocal.start()
    pending = []

    def incoming(k, ph, st):
        i0, i1, order = CLASSES[k]
        dim, done = order[ph], order[:ph]
        half = (i1 - i0) // 2
        if dim == "z":
            return [(part_of(buf, at, done, "z", 1 - at["z"], i0, i1), r_sem.at[k, ph, 0])]
        left, right = ahead(at, dim, -1), ahead(at, dim, 1)
        if st == 0:
            return [
                (part_of(buf, at, done, dim, left, i0, i1), r_sem.at[k, ph, 0]),
                (part_of(buf, at, done, dim, right, i0, i1), r_sem.at[k, ph, 1]),
            ]
        across = ahead(at, dim, 2)
        return [
            (part_of(buf, at, done, dim, across, i0, i0 + half), r_sem.at[k, ph, 2]),
            (part_of(buf, at, done, dim, across, i0 + half, i1), r_sem.at[k, ph, 3]),
        ]

    def await_step(k, ph, st):
        for ref, sem in incoming(k, ph, st):
            remote(ref, ref, s_sem.at[k, ph, 0], sem, partner).wait_recv()

    local_waited = []

    def push(ref_from, ref_to, k, ph, n, to):
        copy = remote(ref_from, ref_to, s_sem.at[k, ph, n], r_sem.at[k, ph, n], to)
        copy.start()
        pending.append(copy)

    def gpush(src, dst, n, to):
        copy = remote(src, dst, g_send.at[8 + n], g_recv.at[8 + n], to)
        copy.start()
        pending.append(copy)

    xr, xl = device(at, x=ahead(at, "x", 1)), device(at, x=ahead(at, "x", -1))
    zo = device(at, z=1 - at["z"])
    gpush(gmine, gbuf.at[at["z"], at["x"]], 0, xr)
    gpush(gmine, gbuf.at[at["z"], at["x"]], 1, xl)

    def gwait(x, z, n):
        ref = gbuf.at[z, x]
        remote(ref, ref, g_send.at[0], g_recv.at[8 + n], partner).wait_recv()

    for k, ph, st in order_gather(CLASSES):
        i0, i1, order = CLASSES[k]
        if st == 1:
            await_step(k, ph, 0)
        elif ph > 0:
            await_step(k, ph - 1, 0 if order[ph - 1] == "z" else 1)
        if ph == 3:
            continue
        dim, done = order[ph], order[:ph]
        half = (i1 - i0) // 2
        if ph > 0 and not local_waited:
            local.wait()
            local_waited.append(1)

        def mine_part(lo, hi):
            if ph == 0:
                return own.at[lo:hi]
            return part_of(buf, at, done, dim, at[dim], lo, hi)

        target = part_of(buf, at, done, dim, at[dim], i0, i1)
        if dim == "z":
            push(mine_part(i0, i1), target, k, ph, 0, zo)
            continue
        right, left = device(at, **{dim: ahead(at, dim, 1)}), device(at, **{dim: ahead(at, dim, -1)})
        if st == 0:
            push(mine_part(i0, i1), target, k, ph, 0, right)
            push(mine_part(i0, i1), target, k, ph, 1, left)
        else:
            a = part_of(buf, at, done, dim, ahead(at, dim, -1), i0, i0 + half)
            b = part_of(buf, at, done, dim, ahead(at, dim, 1), i0 + half, i1)
            push(a, a, k, ph, 2, right)
            push(b, b, k, ph, 3, left)
    swap = remote(buf.at[0, 0:6], other, e_sem.at[0], e_sem.at[1], partner)
    swap.start()
    glocal.wait()
    gwait(ahead(at, "x", -1), at["z"], 0)
    gwait(ahead(at, "x", 1), at["z"], 1)
    fwd = gbuf.at[at["z"], ahead(at, "x", -1)]
    gpush(fwd, fwd, 2, xr)
    gwait(ahead(at, "x", 2), at["z"], 2)
    gpush(gbuf.at[at["z"]], gbuf.at[at["z"]], 3, zo)
    ref = gbuf.at[1 - at["z"]]
    remote(ref, ref, g_send.at[0], g_recv.at[11], partner).wait_recv()
    for copy in pending:
        copy.wait_send()
    tok_local.wait()
    tok.wait_send()
    ref = tok_out.at[1 - at["t"]]
    remote(ref, ref, e_sem.at[2], e_sem.at[3], partner).wait_recv()
    swap.wait()


def gather_all(w, gains, tokens):
    n = len(CLASSES)
    dma = pltpu.SemaphoreType.DMA
    return pl.pallas_call(
        gather_kernel,
        name="gather_weights",
        out_shape=(
            jax.ShapeDtypeStruct((4, 12, 2, 4, ROWS, 128), bf16),
            jax.ShapeDtypeStruct((6, 2, 4, ROWS, 128), bf16),
            jax.ShapeDtypeStruct((2, 4, 8, 128), f32),
            jax.ShapeDtypeStruct((2, *tokens.shape), bf16),
        ),
        in_specs=[VMEM_SPEC] * 9,
        out_specs=[ANY_SPEC] * 4,
        scratch_shapes=[
            pltpu.VMEM((8, 12, SHARD, 128), bf16),
            pltpu.VMEM((8, 12, SHARD, 128), bf16),
            pltpu.VMEM((ROWS, 128), f32),
            pltpu.VMEM((12, ROWS, 128), bf16),
            pltpu.VMEM((8, 8, 128), f32),
            pltpu.VMEM((8, 128), f32),
            dma((8,)),
            dma((8,)),
            dma((12,)),
            dma((12,)),
            dma((n, 3, 4)),
            dma((n, 3, 4)),
            dma((4,)),
            dma((3,)),
        ],
        compiler_params=pltpu.CompilerParams(collective_id=1, has_side_effects=True, vmem_limit_bytes=VMEM_MOST),
    )(*w, gains, tokens)


def order_scatter(classes, rate=46e3, hop=2.5):
    free, events, queue = {}, [], []
    for k in range(len(classes)):
        queue.append((0.0, k, 0, 0))
    while queue:
        queue.sort()
        ready, k, ph, st = queue.pop(0)
        i0, i1, order = classes[k]
        events.append((k, ph, st))
        if ph == len(order):
            continue
        dim, done = order[2 - ph], order[: 2 - ph]
        size = size_of(done, i1 - i0)
        if dim == "z":
            ways, moved, follow = ("z+",), size, (k, ph + 1, 0)
        elif st == 0:
            ways, moved, follow = (dim + "+", dim + "-"), size / 2, (k, ph, 1)
        else:
            ways, moved, follow = (dim + "+", dim + "-"), size, (k, ph + 1, 0)
        end = 0.0
        for way in ways:
            begin = max(ready, free.get(way, 0.0))
            free[way] = begin + (size if dim != "z" and st == 0 else moved if dim == "z" else size / 2) / rate
            end = max(end, begin + (moved if st == 0 else size / 2) / rate)
        queue.append((end + hop, *follow))
    return events


def recv_shape(done, n):
    return (*((4,) if "y" in done else ()), n, *((2,) if "z" in done else ()), *((4,) if "x" in done else ()), ROWS, 128)


def scatter_shapes():
    shapes = []
    for i0, i1, order in CLASSES:
        n = i1 - i0
        for ph in range(3):
            dim, done = order[2 - ph], order[: 2 - ph]
            if dim == "z":
                shapes.append(recv_shape(done, n))
            else:
                shapes.append((4, *recv_shape(done, n // 2)))
                shapes.append((2, *recv_shape(done, n // 2)))
    return shapes


def add_into(acc_part, refs):
    shape = acc_part.shape[:-2]
    total = math.prod(shape)

    @pl.loop(0, total)
    def _(at):
        index, rest = [], at
        for size in reversed(shape):
            index.insert(0, lax.rem(rest, size))
            rest = rest // size
        value = acc_part[tuple(index)].astype(f32)
        for ref in refs:
            value = value + ref[tuple(index)].astype(f32)
        acc_part[tuple(index)] = value.astype(bf16)


def scatter_kernel(
    attn_own, attn_other, ffn, gains,
    q_out, k_out, v_out, o_out, g_out, u_out, d_out, gains_out,
    acc, pair, own32, send, got, gacc, grecv, ggot, kv, kvr, gfin, gfinal, gother, *rest,
):
    lands, (s_sem, r_sem, a_send, a_recv, g_send, g_recv, e_sem, l_sem) = rest[:-8], rest[-8:]
    at = coords()
    group = group_peers(at)
    partner = device(at, c=1 - at["c"])
    mirror = device(at, t=1 - at["t"])
    ring = [device(at, x=ahead(at, "x", 1)), device(at, x=ahead(at, "x", -1)), device(at, z=1 - at["z"])]
    ring.append(device(at, x=ahead(at, "x", 2)))
    loads = []
    for y in range(4):
        if y == 0:
            loads.append(pltpu.make_async_copy(attn_own, acc.at[0, 0:6], l_sem.at[0]))
            loads.append(pltpu.make_async_copy(ffn.at[0:6], acc.at[0, 6:12], l_sem.at[1]))
        else:
            loads.append(pltpu.make_async_copy(ffn.at[12 * y - 6 : 12 * y + 6], acc.at[y], l_sem.at[y + 1]))
    loads.append(pltpu.make_async_copy(gains, gacc, l_sem.at[5]))
    for copy in loads:
        copy.start()
    enter([device(p) for p in group] + ring + [mirror])
    swap = remote(attn_other, pair, e_sem.at[0], e_sem.at[1], partner)
    swap.start()
    pending = []

    def push(src, dst, send_sem, recv_sem, to):
        copy = remote(src, dst, send_sem, recv_sem, to)
        copy.start()
        pending.append(copy)

    for copy in loads:
        copy.wait()
    swap.wait()
    add_into(acc.at[0, 0:6], [pair])

    zo = device(at, z=1 - at["z"])
    push(gacc.at[1 - at["z"]], grecv.at[0:4], g_send.at[8], g_recv.at[8], zo)

    slots, position = {}, 0
    for k, (i0, i1, order) in enumerate(CLASSES):
        for ph in range(3):
            if order[2 - ph] == "z":
                slots[k, ph] = (lands[position],)
                position += 1
            else:
                slots[k, ph] = (lands[position], lands[position + 1])
                position += 2

    def await_ref(ref, sem):
        remote(ref, ref, s_sem.at[0, 0, 0], sem, partner).wait_recv()

    for k, ph, st in order_scatter(CLASSES):
        i0, i1, order = CLASSES[k]
        half = (i1 - i0) // 2
        if st == 0 and ph > 0:
            dim, done = order[3 - ph], order[: 3 - ph]
            if dim == "z":
                (land,) = slots[k, ph - 1]
                await_ref(land, r_sem.at[k, ph - 1, 0])
                add_into(part_of(acc, at, done, "z", at["z"], i0, i1), [land])
            else:
                wide, _ = slots[k, ph - 1]
                for n in range(4):
                    await_ref(wide.at[n], r_sem.at[k, ph - 1, 2 + n])
                add_into(part_of(acc, at, done, dim, at[dim], i0, i0 + half), [wide.at[0], wide.at[2]])
                add_into(part_of(acc, at, done, dim, at[dim], i0 + half, i1), [wide.at[1], wide.at[3]])
        if ph == 3:
            continue
        dim, done = order[2 - ph], order[: 2 - ph]
        if dim == "z":
            (land,) = slots[k, ph]
            push(part_of(acc, at, done, "z", 1 - at["z"], i0, i1), land, s_sem.at[k, ph, 0], r_sem.at[k, ph, 0], zo)
            continue
        right, left = device(at, **{dim: ahead(at, dim, 1)}), device(at, **{dim: ahead(at, dim, -1)})
        wide, narrow = slots[k, ph]
        p1, m1, p2 = ahead(at, dim, 1), ahead(at, dim, -1), ahead(at, dim, 2)
        lo, hi = (i0, i0 + half), (i0 + half, i1)

        def sem(n):
            return s_sem.at[k, ph, n], r_sem.at[k, ph, n]

        if st == 0:
            push(part_of(acc, at, done, dim, p2, *lo), narrow.at[0], *sem(0), right)
            push(part_of(acc, at, done, dim, p2, *hi), narrow.at[1], *sem(1), left)
            push(part_of(acc, at, done, dim, p1, *hi), wide.at[1], *sem(3), right)
            push(part_of(acc, at, done, dim, m1, *lo), wide.at[2], *sem(4), left)
        else:
            await_ref(narrow.at[0], r_sem.at[k, ph, 0])
            add_into(part_of(acc, at, done, dim, p1, *lo), [narrow.at[0]])
            push(part_of(acc, at, done, dim, p1, *lo), wide.at[0], *sem(2), right)
            await_ref(narrow.at[1], r_sem.at[k, ph, 1])
            add_into(part_of(acc, at, done, dim, m1, *hi), [narrow.at[1]])
            push(part_of(acc, at, done, dim, m1, *hi), wide.at[3], *sem(5), left)

    await_ref(grecv.at[0:4], g_recv.at[8])
    gacc[at["z"]] = gacc[at["z"]] + grecv[0:4]
    for n in range(1, 4):
        xx = ahead(at, "x", n)
        push(gacc.at[at["z"], xx], grecv.at[4 + n], g_send.at[8 + n], g_recv.at[8 + n], device(at, x=xx))

    mine = at["y"] * 2 + at["c"]
    me = slot_of(at)

    @pl.loop(0, 12)
    def _(i):
        own32[...] = acc[at["y"], i, at["z"], at["x"]].astype(f32)
        for s in range(8):
            send[s, i] = own32[SHARD * s : SHARD * (s + 1), :].astype(bf16)

    for n, p in enumerate(group):
        s = p["y"] * 2 + p["c"]
        push(send.at[s], got.at[me], a_send.at[n], a_recv.at[me], device(p))
    here = pltpu.make_async_copy(send.at[mine], got.at[me], l_sem.at[0])
    here.start()
    gsum = gacc[at["z"], at["x"]]
    for n in range(1, 4):
        await_ref(grecv.at[4 + n], g_recv.at[8 + n])
        gsum = gsum + grecv[4 + n]
    gfin[...] = gsum
    for n, p in enumerate(group):
        push(gfin, ggot.at[mine], g_send.at[n], g_recv.at[mine], device(p))
    here.wait()
    for p in group:
        ref = got.at[slot_of(p)]
        await_ref(ref, a_recv.at[slot_of(p)])
    ggot[mine] = gsum
    for p in group:
        s = p["y"] * 2 + p["c"]
        await_ref(ggot.at[s], g_recv.at[s])
    total = ggot[0]
    for s in range(1, 8):
        total = total + ggot[s]
    gfinal[...] = total
    outs = {"q": q_out, "o": o_out, "g": g_out, "u": u_out, "d": d_out}
    later = []
    for k, blocks in enumerate(block_sources()):
        for pos, source in enumerate(blocks):
            if source is None:
                continue
            y, i = divmod(pos, 12)
            name, j = source
            if name in "kv":
                j += 2 if name == "v" else 0
                kv[:, j * 128 : (j + 1) * 128] = got[k * 4 + y, i].astype(f32)
            else:
                later.append((name, j, k * 4 + y, i))
    push(kv, kvr, e_sem.at[2], e_sem.at[3], mirror)
    push(gfinal, gother, e_sem.at[4], e_sem.at[5], mirror)
    for name, j, s, i in later:
        outs[name][:, j * 128 : (j + 1) * 128] = got[s, i].astype(f32)
    await_ref(kvr, e_sem.at[3])
    await_ref(gother, e_sem.at[5])
    k_out[...] = kv[:, 0:256] + kvr[:, 0:256]
    v_out[...] = kv[:, 256:512] + kvr[:, 256:512]
    gains_out[...] = gfinal[...] + gother[...]
    for copy in pending:
        copy.wait_send()


def scatter_all(attn_own, attn_other, ffn, gains):
    n = len(CLASSES)
    dma = pltpu.SemaphoreType.DMA
    widths = (512, 256, 256, 512, 3456, 3456, 3456)
    return pl.pallas_call(
        scatter_kernel,
        name="scatter_grads",
        out_shape=tuple(jax.ShapeDtypeStruct((SHARD, w), f32) for w in widths) + (jax.ShapeDtypeStruct((8, 128), f32),),
        in_specs=[ANY_SPEC] * 4,
        out_specs=[VMEM_SPEC] * 8,
        scratch_shapes=[
            pltpu.VMEM((4, 12, 2, 4, ROWS, 128), bf16),
            pltpu.VMEM((6, 2, 4, ROWS, 128), bf16),
            pltpu.VMEM((ROWS, 128), f32),
            pltpu.VMEM((8, 12, SHARD, 128), bf16),
            pltpu.VMEM((8, 12, SHARD, 128), bf16),
            pltpu.VMEM((2, 4, 8, 128), f32),
            pltpu.VMEM((8, 8, 128), f32),
            pltpu.VMEM((8, 8, 128), f32),
            pltpu.VMEM((SHARD, 512), f32),
            pltpu.VMEM((SHARD, 512), f32),
            pltpu.VMEM((8, 128), f32),
            pltpu.VMEM((8, 128), f32),
            pltpu.VMEM((8, 128), f32),
            *[pltpu.VMEM(s, bf16) for s in scatter_shapes()],
            dma((n, 3, 6)),
            dma((n, 3, 6)),
            dma((8,)),
            dma((8,)),
            dma((12,)),
            dma((12,)),
            dma((6,)),
            dma((6,)),
        ],
        compiler_params=pltpu.CompilerParams(collective_id=2, has_side_effects=True, vmem_limit_bytes=VMEM_MOST),
    )(attn_own, attn_other, ffn, gains)


def pair_kernel(reduce, src, out, stage, land, send_sem, recv_sem, local_sem):
    at = coords()
    mirror = device(at, t=1 - at["t"])
    mine = pl.ds(pl.multiple_of(at["t"] * 128, 128), 128)
    theirs = pl.ds(pl.multiple_of((1 - at["t"]) * 128, 128), 128)
    if reduce:
        stage[...] = src[theirs, :].astype(bf16)
        enter([mirror])
        copy = remote(stage, land, send_sem, recv_sem, mirror)
        copy.start()
        copy.wait()
        out[...] = src[mine, :] + land[...].astype(f32)
    else:
        enter([mirror])
        copy = remote(src, land, send_sem, recv_sem, mirror)
        copy.start()
        out[mine, :] = src[...]
        copy.wait()
        out[theirs, :] = land[...]


def pair_call(value, reduce, number):
    rows, width = value.shape
    dma = pltpu.SemaphoreType.DMA
    out = (rows // 2, width) if reduce else (rows * 2, width)
    return pl.pallas_call(
        functools.partial(pair_kernel, reduce),
        name="pair_sum" if reduce else "pair_gather",
        out_shape=jax.ShapeDtypeStruct(out, f32 if reduce else bf16),
        in_specs=[VMEM_SPEC],
        out_specs=VMEM_SPEC,
        scratch_shapes=[pltpu.VMEM((128, width), bf16), pltpu.VMEM((128, width), bf16), dma, dma, dma],
        compiler_params=pltpu.CompilerParams(collective_id=number, has_side_effects=True),
    )(value)


def ffn_kernel(
    x_in, res, cot, gain, buf,
    out, d_in, gpp, grads,
    w, dw, xs, ds, xt, dt, gates, ups, part, land_a, land_b, zstage, zland_a, zland_b,
    w_sem, dw_sem, s_sem, r_sem,
):
    at = coords()
    mirror = device(at, t=1 - at["t"])
    partner = device(at, c=1 - at["c"])
    pairs = 7
    loads = []
    for j in range(pairs):
        for n in range(3):
            lo = n * 14 + 2 * j
            copy = pltpu.make_async_copy(buf.at[6 + lo : 8 + lo], w.at[lo : lo + 2], w_sem.at[j, n])
            copy.start()

    def rows(c, t, n=1):
        return pl.ds(pl.multiple_of((c * 2 + t) * 128, 128), 128 * n)

    enter([mirror, partner])
    c, t = at["c"], at["t"]

    def gather(e, full):
        view = lambda cc, tt: full.at[rows(cc, tt), :]
        a = remote(view(c, t), view(c, t), s_sem.at[e, 0], r_sem.at[e, 0], mirror)
        b = remote(view(c, t), view(c, t), s_sem.at[e, 1], r_sem.at[e, 1], partner)
        a.start()
        b.start()
        ref = view(c, 1 - t)
        remote(ref, ref, s_sem.at[e, 0], r_sem.at[e, 0], mirror).wait_recv()
        f = remote(ref, ref, s_sem.at[e, 2], r_sem.at[e, 2], partner)
        f.start()
        one, two = view(1 - c, t), view(1 - c, 1 - t)
        remote(one, one, s_sem.at[e, 0], r_sem.at[e, 1], mirror).wait_recv()
        remote(two, two, s_sem.at[e, 0], r_sem.at[e, 2], mirror).wait_recv()
        for copy in (a, b, f):
            copy.wait_send()

    def reduce(e, land, zland):
        a = remote(part.at[rows(1 - c, 0, 2), :], land, s_sem.at[e, 0], r_sem.at[e, 0], partner)
        a.start()
        a.wait()
        far = pl.ds(pl.multiple_of((1 - t) * 128, 128), 128)
        near = pl.ds(pl.multiple_of(t * 128, 128), 128)
        zstage[...] = (part[rows(c, 1 - t), :] + land[far, :]).astype(bf16)
        b = remote(zstage, zland, s_sem.at[e, 1], r_sem.at[e, 1], mirror)
        b.start()
        kept = part[rows(c, t), :] + land[near, :]
        b.wait()
        return kept + zland[...].astype(f32)

    xs[rows(c, t), :] = x_in[...]
    gather(0, xs)
    part[...] = jnp.zeros_like(part)

    def weights(j, n):
        return jnp.concatenate([w[n * 14 + 2 * j], w[n * 14 + 2 * j + 1]], axis=1)

    def rows_dot(a, b):
        return lax.dot_general(a, b, (((1,), (1,)), ((), ())), preferred_element_type=f32)

    @pl.loop(0, pairs)
    def _(j):
        lanes = pl.ds(pl.multiple_of(j * 256, 256), 256)
        for n in range(3):
            pltpu.make_async_copy(buf.at[0:2], w.at[0:2], w_sem.at[j, n]).wait()
        gate = jnp.dot(xs[...], weights(j, 0), preferred_element_type=f32)
        up = jnp.dot(xs[...], weights(j, 1), preferred_element_type=f32)
        gates[:, lanes] = gate
        ups[:, lanes] = up
        act = 0.5 * gate * (1.0 + jnp.tanh(gelu_scale * (gate + gelu_cube * gate * gate * gate)))
        hidden = (act * up).astype(bf16)
        part[...] += rows_dot(hidden, weights(j, 2))

    raw = reduce(1, land_a, zland_a)
    width = raw.shape[1]
    inverse = lax.rsqrt(jnp.sum(raw * raw, axis=-1, keepdims=True) * (1.0 / width) + eps)
    gained = 1.0 + gain[...]
    out[...] = (res[...] + raw * inverse * gained).astype(bf16)
    g = cot[...].astype(f32)
    scaled = g * gained
    mean = jnp.sum(scaled * raw, axis=-1, keepdims=True) * (1.0 / width)
    ds[rows(c, t), :] = (inverse * scaled - raw * inverse * inverse * inverse * mean).astype(bf16)
    gpp[...] = jnp.sum(g * raw * inverse, axis=0, keepdims=True)
    gather(2, ds)
    xt[...] = xs[...].T
    dt[...] = ds[...].T
    part[...] = jnp.zeros_like(part)

    @pl.loop(0, pairs)
    def _(j):
        lanes = pl.ds(pl.multiple_of(j * 256, 256), 256)
        gate, up = gates[:, lanes], ups[:, lanes]
        d_hidden = jnp.dot(ds[...], weights(j, 2), preferred_element_type=f32)
        tanh = jnp.tanh(gelu_scale * (gate + gelu_cube * gate * gate * gate))
        act = 0.5 * gate * (1.0 + tanh)
        slope = 0.5 * (1.0 + tanh) + 0.5 * gate * (1.0 - tanh * tanh) * gelu_scale * (
            1.0 + 3.0 * gelu_cube * gate * gate
        )
        hidden = (act * up).astype(bf16)
        d_gate = (d_hidden * up * slope).astype(bf16)
        d_up = (d_hidden * act).astype(bf16)
        part[...] += rows_dot(d_gate, weights(j, 0)) + rows_dot(d_up, weights(j, 1))
        for n, (left, right) in enumerate(((xt, d_gate), (xt, d_up), (dt, hidden))):
            grad = jnp.dot(left[...], right, preferred_element_type=f32).astype(bf16)
            lo = n * 14 + 2 * j
            dw[lo] = grad[:, :128]
            dw[lo + 1] = grad[:, 128:]
            pltpu.make_async_copy(dw.at[pl.ds(lo, 2)], grads.at[pl.ds(lo, 2)], dw_sem.at[j, n]).start()

    d_in[...] = reduce(3, land_b, zland_b)
    for j in range(pairs):
        for n in range(3):
            lo = n * 14 + 2 * j
            pltpu.make_async_copy(dw.at[lo : lo + 2], grads.at[lo : lo + 2], dw_sem.at[j, n]).wait()


def ffn_all(x_in, res, cot, gain, buf):
    dma = pltpu.SemaphoreType.DMA
    tokens, width = x_in.shape
    return pl.pallas_call(
        ffn_kernel,
        name="ffn_layer",
        out_shape=(
            jax.ShapeDtypeStruct((tokens, width), bf16),
            jax.ShapeDtypeStruct((tokens, width), f32),
            jax.ShapeDtypeStruct((1, width), f32),
            jax.ShapeDtypeStruct((42, width, 128), bf16),
        ),
        in_specs=[VMEM_SPEC] * 4 + [ANY_SPEC],
        out_specs=[VMEM_SPEC] * 3 + [ANY_SPEC],
        scratch_shapes=[
            pltpu.VMEM((42, width, 128), bf16),
            pltpu.VMEM((42, width, 128), bf16),
            pltpu.VMEM((512, width), bf16),
            pltpu.VMEM((512, width), bf16),
            pltpu.VMEM((width, 512), bf16),
            pltpu.VMEM((width, 512), bf16),
            pltpu.VMEM((512, 1792), f32),
            pltpu.VMEM((512, 1792), f32),
            pltpu.VMEM((512, width), f32),
            pltpu.VMEM((256, width), f32),
            pltpu.VMEM((256, width), f32),
            pltpu.VMEM((128, width), bf16),
            pltpu.VMEM((128, width), bf16),
            pltpu.VMEM((128, width), bf16),
            dma((7, 3)),
            dma((7, 3)),
            dma((4, 3)),
            dma((4, 3)),
        ],
        compiler_params=pltpu.CompilerParams(collective_id=3, has_side_effects=True, vmem_limit_bytes=VMEM_MOST),
    )(x_in, res, cot, gain, buf)


def local(
    tokens,
    segment_ids,
    w_query,
    w_key,
    w_value,
    w_out,
    gain_query,
    gain_key,
    gain_pre_attn,
    gain_post_attn,
    w_gate,
    w_up,
    w_down,
    gain_pre_ffn,
    gain_post_ffn,
    cotangent,
):
    my_dp, my_t = lax.axis_index("dp"), lax.axis_index("tensor")
    core = lax.rem(my_dp, 2)
    packed = jnp.concatenate(
        [gain_pre_attn, gain_post_attn, gain_pre_ffn, gain_post_ffn, gain_query, gain_key]
    ).astype(f32)
    packed = jnp.broadcast_to(jnp.pad(packed, (0, 48))[None], (8, 128))
    buf, other, all_gains, both_tokens = gather_all(
        (w_query, w_key, w_value, w_out, w_gate, w_up, w_down), packed, tokens
    )
    width = tokens.shape[1]
    buf = buf.reshape(48, width, 128)
    mine, other = buf[:6], other.reshape(6, width, 128)

    def matrix(blocks):
        return jnp.moveaxis(blocks, 0, 1).reshape(width, -1)

    first = jnp.where(core == 0, mine, other)
    second = jnp.where(core == 0, other, mine)
    query_mat, key_mat = matrix(first[:4]), matrix(first[4:])
    value_mat, out_mat = matrix(second[:2]), matrix(second[2:])
    all_gains = all_gains.reshape(64, 128)
    gain_pa, gain_po, gain_pf, gain_pp = [all_gains[:, 18 * n : 18 * n + 18].reshape(width) for n in range(4)]
    gain_q, gain_k = [all_gains[:, 72 + 4 * n : 76 + 4 * n].reshape(256) for n in range(2)]
    head_size = key_mat.shape[1]
    heads_local = query_mat.shape[1] // head_size
    resid_in = tokens.astype(f32)
    r_one = lax.rsqrt(jnp.mean(resid_in * resid_in, axis=-1, keepdims=True) + eps)
    attn_in = rms_apply(both_tokens.reshape(-1, width).astype(f32), gain_pa)[0].astype(bf16)
    row_count = attn_in.shape[0]
    segment_row = segment_ids[0]
    position = positions_of(segment_row)
    allowed = build_allowed(segment_row)
    query_raw = jnp.dot(attn_in, query_mat, preferred_element_type=f32).reshape(
        row_count, heads_local, head_size
    )
    key_raw = jnp.dot(attn_in, key_mat, preferred_element_type=f32)
    value_vec = jnp.dot(attn_in, value_mat, preferred_element_type=f32).astype(bf16)
    query_norm, r_query = rms_apply(query_raw, gain_q)
    key_norm, r_key = rms_apply(key_raw, gain_k)
    cosine_table, sine_table = rope_tables(position, head_size)
    query_rot = (
        query_norm * cosine_table[:, None, :] + rotate_half(query_norm) * sine_table[:, None, :]
    ).astype(bf16)
    key_rot = (key_norm * cosine_table + rotate_half(key_norm) * sine_table).astype(bf16)
    score_scale = head_size ** (-0.5)
    scores = jnp.einsum("qhd,kd->hqk", query_rot, key_rot, preferred_element_type=f32) * score_scale
    scores = jnp.where(allowed[None], scores, -jnp.inf)
    row_max = jnp.max(scores, axis=-1, keepdims=True)
    row_total = jnp.sum(jnp.exp(scores - row_max), axis=-1, keepdims=True)
    log_total = row_max + jnp.log(row_total)
    weights_full = jnp.where(allowed[None], jnp.exp(scores - log_total), 0.0)
    probs = weights_full.astype(bf16)
    context = (
        jnp.einsum("hqk,kd->qhd", probs, value_vec, preferred_element_type=f32)
        .astype(bf16)
        .reshape(row_count, heads_local * head_size)
    )
    attn_part = jnp.einsum("te,de->td", context, out_mat, preferred_element_type=f32)
    attn_raw = pair_call(attn_part, True, 4)
    attn_normed, r_two = rms_apply(attn_raw, gain_po)
    residual = resid_in + attn_normed
    ffn_local, r_three = rms_apply(residual, gain_pf)
    output, d_ffn_input, grad_gpp, ffn_grads = ffn_all(
        ffn_local.astype(bf16), residual, cotangent, gain_pp[None], buf
    )
    grad_out = cotangent.astype(f32)
    d_resid_norm, grad_gpf = rms_back(residual, r_three, gain_pf, d_ffn_input)
    d_residual = grad_out + d_resid_norm
    d_attn_local, grad_gpo = rms_back(attn_raw, r_two, gain_po, d_residual)
    d_attn_raw = pair_call(d_attn_local.astype(bf16), False, 5)
    d_context = jnp.dot(d_attn_raw, out_mat, preferred_element_type=f32).astype(bf16)
    grad_out_mat = jnp.einsum("td,te->de", d_attn_raw, context, preferred_element_type=f32)
    d_context = d_context.reshape(row_count, heads_local, head_size)
    d_prob = jnp.einsum("qhd,kd->hqk", d_context, value_vec, preferred_element_type=f32)
    delta = jnp.sum(weights_full * d_prob, axis=-1, keepdims=True)
    d_score = (weights_full * (d_prob - delta) * score_scale).astype(bf16)
    d_query_rot = jnp.einsum("hqk,kd->qhd", d_score, key_rot, preferred_element_type=f32)
    d_query_norm = d_query_rot * cosine_table[:, None, :] - rotate_half(
        d_query_rot * sine_table[:, None, :]
    )
    d_query, grad_gq = rms_back(query_raw, r_query, gain_q, d_query_norm)
    d_query = d_query.astype(bf16).reshape(row_count, heads_local * head_size)
    d_key_rot = jnp.einsum("hqk,qhd->kd", d_score, query_rot, preferred_element_type=f32)
    d_key_norm = d_key_rot * cosine_table - rotate_half(d_key_rot * sine_table)
    d_key, grad_gk = rms_back(key_raw, r_key, gain_k, d_key_norm)
    d_key = d_key.astype(bf16)
    d_value = jnp.einsum("hqk,qhd->kd", probs, d_context, preferred_element_type=f32).astype(bf16)
    d_in_part = jnp.einsum("te,de->td", d_query, query_mat, preferred_element_type=f32)
    d_in_part = d_in_part + jnp.einsum("te,de->td", d_key, key_mat, preferred_element_type=f32)
    d_in_part = d_in_part + jnp.einsum("te,de->td", d_value, value_mat, preferred_element_type=f32)
    d_attn_in = pair_call(d_in_part, True, 6)
    grad_query = jnp.einsum("td,te->de", attn_in, d_query, preferred_element_type=f32)
    grad_key = jnp.einsum("td,te->de", attn_in, d_key, preferred_element_type=f32)
    grad_value = jnp.einsum("td,te->de", attn_in, d_value, preferred_element_type=f32)
    d_input_norm, grad_gpa = rms_back(resid_in, r_one, gain_pa, d_attn_in)
    grad_tokens = d_residual + d_input_norm

    def blocks(grad):
        return jnp.moveaxis(grad.astype(bf16).reshape(width, -1, 128), 1, 0)

    one = jnp.concatenate([blocks(grad_query), blocks(grad_key)])
    two = jnp.concatenate([blocks(grad_value), blocks(grad_out_mat)])
    shape = (6, 2, 4, ROWS, 128)
    attn_own = jnp.where(core == 0, one, two).reshape(shape)
    attn_other = jnp.where(core == 0, two, one).reshape(shape)
    small = [g.reshape(64, 18) for g in (grad_gpa, grad_gpo, grad_gpf, grad_gpp)]
    small += [g.reshape(64, 4) for g in (grad_gq, grad_gk)]
    small = jnp.pad(jnp.concatenate(small, axis=1), ((0, 0), (0, 48))).reshape(2, 4, 8, 128)
    sums = scatter_all(attn_own, attn_other, ffn_grads.reshape(42, 2, 4, ROWS, 128), small)
    s_query, s_key, s_value, s_out, s_gate, s_up, s_down, s_gains = sums
    s_gains = lax.dynamic_index_in_dim(s_gains, lax.rem(my_dp, 8), 0, keepdims=False)
    s_pa, s_po, s_pf, s_pp = [s_gains[18 * n : 18 * n + 18] for n in range(4)]
    return (
        output, grad_tokens, s_query, s_key, s_value, s_out, s_gains[72:76], s_gains[76:80],
        s_pa, s_po, s_gate, s_up, s_down, s_pf, s_pp,
    )


def solution(mesh):
    return jax.shard_map(
        local,
        mesh=mesh,
        in_specs=(
            P(("dp", "tensor"), None),
            P("dp", None),
            P("dp", "tensor"),
            P("dp", None),
            P("dp", None),
            P("dp", "tensor"),
            P("dp"),
            P("dp"),
            P("dp"),
            P("dp"),
            P("dp", "tensor"),
            P("dp", "tensor"),
            P("dp", "tensor"),
            P("dp"),
            P("dp"),
            P(("dp", "tensor"), None),
        ),
        out_specs=(
            P(("dp", "tensor"), None),
            P(("dp", "tensor"), None),
            P("dp", "tensor"),
            P("dp", None),
            P("dp", None),
            P("dp", "tensor"),
            P("dp"),
            P("dp"),
            P("dp"),
            P("dp"),
            P("dp", "tensor"),
            P("dp", "tensor"),
            P("dp", "tensor"),
            P("dp"),
            P("dp"),
        ),
        check_vma=False,
    )
```

```python
import functools
import math

import jax
import jax.numpy as jnp
from jax import lax
from jax.experimental import pallas as pl
from jax.experimental.pallas import tpu as pltpu
from jax.sharding import PartitionSpec as P

eps = 1e-06
gelu_scale = 0.7978845608028654
gelu_cube = 0.044715


def positions_of(segment_row):
    token_index = jnp.arange(segment_row.shape[0], dtype=jnp.int32)
    earlier = jnp.concatenate([segment_row[:1] - 1, segment_row[:-1]])
    starts = lax.cummax(jnp.where(segment_row != earlier, token_index, 0), axis=0)
    return token_index - starts


def build_allowed(segment_row):
    token_index = jnp.arange(segment_row.shape[0], dtype=jnp.int32)
    same_seq = segment_row[:, None] == segment_row[None, :]
    causal = token_index[None, :] <= token_index[:, None]
    return same_seq & causal


def rope_tables(position, width):
    half_width = width // 2
    frequency = jnp.exp(
        jnp.arange(half_width, dtype=jnp.float32) * (-2.0 * math.log(10000.0) / width)
    )
    angles = position.astype(jnp.float32)[:, None] * frequency[None, :]
    cosine_table = jnp.concatenate([jnp.cos(angles), jnp.cos(angles)], axis=1)
    sine_table = jnp.concatenate([jnp.sin(angles), jnp.sin(angles)], axis=1)
    return (cosine_table, sine_table)


f32 = jnp.float32
bf16 = jnp.bfloat16
MESH = pl.DeviceIdType.MESH
ROWS = 144
SHARD = 18
VMEM_SPEC = pl.BlockSpec(memory_space=pltpu.VMEM)
ANY_SPEC = pl.BlockSpec(memory_space=pl.ANY)
VMEM_MOST = 66_000_000

CLASSES = (
    (0, 1, "zxy"),
    (1, 2, "zyx"),
    (2, 4, "zxy"),
    (4, 6, "zyx"),
    (6, 8, "zxy"),
    (8, 10, "zyx"),
    (10, 11, "xyz"),
    (11, 12, "yxz"),
)
ATTN_CLASSES = (0, 1)
ROW_CUT = 80


def place(block):
    return block // 10 * 12 + 2 + block % 10 if block < 30 else 6 + block


def attn_place(block):
    return block // 2 * 12 + block % 2


def coords():
    dp, t = lax.axis_index("dp"), lax.axis_index("tensor")
    return {"c": lax.rem(dp, 2), "y": lax.rem(dp // 2, 4), "x": lax.rem(dp // 8, 4), "z": dp // 32, "t": t}


def device(at, **change):
    p = {**at, **change}
    return (((p["z"] * 4 + p["x"]) * 4 + p["y"]) * 2 + p["c"], p["t"])


def ahead(at, dim, by):
    size = 2 if dim == "z" else 4
    return lax.rem(at[dim] + by + size, size)


def block_sources():
    attn = [("q", j) for j in range(4)] + [("k", j) for j in range(2)]
    attn_two = [("v", j) for j in range(2)] + [("o", j) for j in range(4)]
    ffn = [[(n, j) for n in "gud" for j in range(14)], [(n, j + 14) if j < 13 else None for n in "gud" for j in range(14)]]
    cores = []
    for small, large in ((attn, ffn[0]), (attn_two, ffn[1])):
        spots = [None] * 48
        for n, source in enumerate(small):
            spots[attn_place(n)] = source
        for n, source in enumerate(large):
            spots[place(n)] = source
        cores.append(spots)
    return cores


def enter(peers):
    barrier = pltpu.get_barrier_semaphore()
    for peer in peers:
        pl.semaphore_signal(barrier, inc=1, device_id=peer, device_id_type=MESH)
    pl.semaphore_wait(barrier, len(peers))


def remote(src, dst, send, recv, to):
    return pltpu.make_async_remote_copy(
        src_ref=src, dst_ref=dst, send_sem=send, recv_sem=recv, device_id=to, device_id_type=MESH
    )


def group_peers(at):
    peers = []
    for dy in range(4):
        for dc in range(2):
            if dy or dc:
                peers.append({**at, "y": ahead(at, "y", dy), "c": lax.rem(at["c"] + dc, 2)})
    return peers


def slot_of(p):
    return p["c"] * 4 + p["y"]


def part_of(buf, at, done, dim, index, i0, i1, side=None):
    pick = {d: (slice(None) if d in done else at[d]) for d in "zxy"}
    if dim is not None:
        pick[dim] = index
    (lo, hi), rows = side_of(i0, i1, side)
    return buf.at[pick["y"], lo:hi, pick["z"], pick["x"], rows[0] : rows[1]]


def side_of(i0, i1, side):
    n = i1 - i0
    if side is None:
        return (i0, i1), (0, ROWS)
    if n % 2 == 0:
        mid = i0 + n // 2
        return ((i0, mid), (mid, i1))[side], (0, ROWS)
    return (i0, i1), ((0, ROW_CUT), (ROW_CUT, ROWS))[side]


def size_of(done, n):
    size = n * ROWS * 128 * 2
    for d in done:
        size *= 2 if d == "z" else 4
    return size


def order_gather(classes, early, pieces, rate=46e3, hop=1.6):
    free, events, queue = {}, [], []
    left = len(early)
    for k in range(len(classes)):
        queue.append((0.0, k, 0, 0))
    while queue:
        queue.sort()
        ready, k, ph, st = queue.pop(0)
        if k < 0:
            events.append((ph,))
            continue
        i0, i1, order = classes[k]
        events.append((k, ph, st))
        if ph == len(order):
            left -= k in early
            if k in early and not left:
                queue += [(ready + t, -1, n, 0) for n, t in enumerate(pieces)]
            continue
        dim, done = order[ph], order[:ph]
        size = size_of(done, i1 - i0)
        if dim == "z":
            ways, moved, follow = ("z+",), size, (k, ph + 1, 0)
        elif st == 0:
            ways, moved, follow = (dim + "+", dim + "-"), size, (k, ph, 1)
        else:
            ways, moved, follow = (dim + "+", dim + "-"), size / 2, (k, ph + 1, 0)
        end = 0.0
        for way in ways:
            free[way] = max(ready, free.get(way, 0.0)) + moved / rate
            end = max(end, free[way])
        queue.append((end + hop, *follow))
    return events


def normed(values, gain):
    inverse = lax.rsqrt(jnp.mean(values * values, axis=-1, keepdims=True) + eps)
    return values * inverse * (1.0 + gain), inverse


def norm_back(values, gain, grad):
    inverse = lax.rsqrt(jnp.mean(values * values, axis=-1, keepdims=True) + eps)
    scaled = grad * (1.0 + gain)
    mean = jnp.mean(scaled * values, axis=-1, keepdims=True)
    back = inverse * scaled - values * inverse * inverse * inverse * mean
    return back, jnp.sum(grad * values * inverse, axis=0, keepdims=True)


def half_turn(values):
    return jnp.concatenate([-values[:, 128:], values[:, :128]], axis=1)


def last_dot(a, b):
    return lax.dot_general(a, b, (((1,), (1,)), ((), ())), preferred_element_type=f32)


def spread_marks(each, offset, width):
    lane = lax.broadcasted_iota(jnp.int32, (128, width), 0)
    entry = lax.broadcasted_iota(jnp.int32, (128, width), 1)
    picks = lane == offset + lax.rem(entry, each)
    dev = lax.broadcasted_iota(jnp.int32, (64, width), 0)
    owns = lax.div(lax.broadcasted_iota(jnp.int32, (64, width), 1), each) == dev
    return picks, owns


def spread_gains(gbuf, gain_d, gain_h):
    tile = gbuf[...].reshape(64, 128).astype(bf16)
    for n in range(4):
        picks, owns = spread_marks(SHARD, SHARD * n, gain_d.shape[1])
        wide = jnp.dot(tile, picks.astype(f32).astype(bf16), preferred_element_type=f32)
        gain_d[n : n + 1, :] = jnp.sum(jnp.where(owns, wide, 0.0), axis=0, keepdims=True)
    for n in range(2):
        picks, owns = spread_marks(4, 4 * SHARD + 4 * n, 256)
        wide = jnp.dot(tile, picks.astype(f32).astype(bf16), preferred_element_type=f32)
        gain_h[n : n + 1, :] = jnp.sum(jnp.where(owns, wide, 0.0), axis=0, keepdims=True)


def fold_gains(grads_d, grads_h):
    total = jnp.zeros((64, 128), f32)
    for n in range(4):
        picks, owns = spread_marks(SHARD, SHARD * n, grads_d[n].shape[1])
        wide = jnp.where(owns, grads_d[n], 0.0)
        total += lax.dot_general(
            wide, picks.astype(f32), (((1,), (1,)), ((), ())),
            precision=lax.Precision.HIGHEST, preferred_element_type=f32,
        )
    for n in range(2):
        picks, owns = spread_marks(4, 4 * SHARD + 4 * n, 256)
        wide = jnp.where(owns, grads_h[n], 0.0)
        total += lax.dot_general(
            wide, picks.astype(f32), (((1,), (1,)), ((), ())),
            precision=lax.Precision.HIGHEST, preferred_element_type=f32,
        )
    return total


def blocks_of(w, first, count):
    width = 8 * ROWS
    return jnp.concatenate([w[first + n].reshape(width, 128) for n in range(count)], axis=1)


def attn_forward(at, attn_in, w, cos, sin, allowed, q_raw, k_raw, value, q_rot, k_rot, soft, context, part, gain_h):
    def queries():
        q_raw[...] = jnp.dot(attn_in[...], blocks_of(w, 0, 4), preferred_element_type=f32)
        for h in range(2):
            lanes = slice(256 * h, 256 * h + 256)
            q = normed(q_raw[:, lanes], gain_h[0:1, :])[0]
            q_rot[:, lanes] = (q * cos[...] + half_turn(q) * sin[...]).astype(bf16)

    def keys():
        key = jnp.dot(attn_in[...], blocks_of(w, 4, 2), preferred_element_type=f32)
        k_raw[...] = key
        key = normed(key, gain_h[1:2, :])[0]
        k_rot[...] = (key * cos[...] + half_turn(key) * sin[...]).astype(bf16)
        value[...] = jnp.dot(attn_in[...], blocks_of(w, 6, 2), preferred_element_type=f32).astype(bf16)

    def heads():
        seen = allowed[...] > 0.0
        for h in range(2):
            lanes = slice(256 * h, 256 * h + 256)
            scores = last_dot(q_rot[:, lanes], k_rot[...]) * (256.0 ** -0.5)
            scores = jnp.where(seen, scores, -jnp.inf)
            top = jnp.max(scores, axis=-1, keepdims=True)
            total = jnp.sum(jnp.exp(scores - top), axis=-1, keepdims=True)
            full = jnp.where(seen, jnp.exp(scores - (top + jnp.log(total))), 0.0)
            soft[h] = full
            context[:, lanes] = jnp.dot(full.astype(bf16), value[...], preferred_element_type=f32).astype(bf16)

    def project():
        part[...] = last_dot(context[...], blocks_of(w, 8, 4))

    return [queries, keys, heads, project]


def gather_kernel(
    q_ref, k_ref, v_ref, o_ref, g_ref, u_ref, d_ref, gains_ref, tok_ref, cos_ref, sin_ref, allowed_ref,
    buf, other, attn_in, q_raw, k_raw, value, q_rot, k_rot, soft, context, attn_raw, residual, ffn_in, gain_d, gain_h,
    send, got, own32, own, ggot, gmine, gbuf, tok_out, w, part, pstage, pland,
    a_send, a_recv, g_send, g_recv, s_sem, r_sem, e_sem, l_sem, w_sem,
):
    at = coords()
    refs = {"q": q_ref, "k": k_ref, "v": v_ref, "o": o_ref, "g": g_ref, "u": u_ref, "d": d_ref}
    group = group_peers(at)
    partner = device(at, c=1 - at["c"])
    mirror = device(at, t=1 - at["t"])
    ring = [device(at, x=ahead(at, "x", 1)), device(at, x=ahead(at, "x", -1)), device(at, z=1 - at["z"])]
    for k, blocks in enumerate(block_sources()):
        for pos, source in enumerate(blocks):
            y, i = divmod(pos, 12)
            if source is None:
                send[k * 4 + y, i] = jnp.zeros((SHARD, 128), bf16)
            else:
                name, j = source
                send[k * 4 + y, i] = refs[name][:, j * 128 : (j + 1) * 128]
    row = lax.broadcasted_iota(jnp.int32, (8, 128), 0)
    gmine[...] = jnp.where(row == at["y"] * 2 + at["c"], gains_ref[...], 0.0)
    me = slot_of(at)
    mine = at["y"] * 2 + at["c"]
    enter([device(p) for p in group] + ring + [mirror])
    tok = remote(tok_ref, tok_out.at[at["t"]], e_sem.at[2], e_sem.at[3], mirror)
    tok.start()
    tok_local = pltpu.make_async_copy(tok_ref, tok_out.at[at["t"]], l_sem.at[1])
    tok_local.start()
    first = []
    for n, p in enumerate(group):
        copy = remote(send.at[slot_of(p)], got.at[mine], a_send.at[n], a_recv.at[mine], device(p))
        small = remote(gmine, ggot.at[mine], g_send.at[n], g_recv.at[mine], device(p))
        copy.start()
        small.start()
        first += [copy, small]
    here = pltpu.make_async_copy(send.at[me], got.at[mine], l_sem.at[0])
    here.start()
    here.wait()
    for p in group:
        s = p["y"] * 2 + p["c"]
        remote(send.at[0], got.at[s], a_send.at[0], a_recv.at[s], device(p)).wait_recv()
        remote(gmine, ggot.at[s], g_send.at[0], g_recv.at[s], device(p)).wait_recv()
    ggot[mine] = gmine[...]
    gmine_sum = ggot[0]
    for s in range(1, 8):
        gmine_sum = gmine_sum + ggot[s]

    @pl.loop(0, 12)
    def _(i):
        for s in range(8):
            own32[SHARD * s : SHARD * (s + 1), :] = got[s, i].astype(f32)
        own[i] = own32[...].astype(bf16)

    for copy in first:
        copy.wait_send()
    gmine[...] = gmine_sum
    local = pltpu.make_async_copy(own, part_of(buf, at, "", None, None, 0, 12), l_sem.at[0])
    local.start()
    glocal = pltpu.make_async_copy(gmine, gbuf.at[at["z"], at["x"]], l_sem.at[2])
    glocal.start()
    pending = []

    def incoming(k, ph, st):
        i0, i1, order = CLASSES[k]
        dim, done = order[ph], order[:ph]
        if dim == "z":
            return [(part_of(buf, at, done, "z", 1 - at["z"], i0, i1), r_sem.at[k, ph, 0])]
        left, right = ahead(at, dim, -1), ahead(at, dim, 1)
        if st == 0:
            return [
                (part_of(buf, at, done, dim, left, i0, i1), r_sem.at[k, ph, 0]),
                (part_of(buf, at, done, dim, right, i0, i1), r_sem.at[k, ph, 1]),
            ]
        across = ahead(at, dim, 2)
        return [
            (part_of(buf, at, done, dim, across, i0, i1, 0), r_sem.at[k, ph, 2]),
            (part_of(buf, at, done, dim, across, i0, i1, 1), r_sem.at[k, ph, 3]),
        ]

    def await_step(k, ph, st):
        for ref, sem in incoming(k, ph, st):
            remote(ref, ref, s_sem.at[k, ph, 0], sem, partner).wait_recv()

    local_waited = []

    def push(ref_from, ref_to, k, ph, n, to):
        copy = remote(ref_from, ref_to, s_sem.at[k, ph, n], r_sem.at[k, ph, n], to)
        copy.start()
        pending.append(copy)

    def gpush(src, dst, n, to):
        copy = remote(src, dst, g_send.at[8 + n], g_recv.at[8 + n], to)
        copy.start()
        pending.append(copy)

    xr, xl = device(at, x=ahead(at, "x", 1)), device(at, x=ahead(at, "x", -1))
    zo = device(at, z=1 - at["z"])
    gpush(gmine, gbuf.at[at["z"], at["x"]], 0, xr)
    gpush(gmine, gbuf.at[at["z"], at["x"]], 1, xl)

    def gwait(x, z, n):
        ref = gbuf.at[z, x]
        remote(ref, ref, g_send.at[0], g_recv.at[8 + n], partner).wait_recv()

    pair_copy = remote(pstage, pland, e_sem.at[4], e_sem.at[5], mirror)
    swaps = [remote(buf.at[y, 0:2], other.at[y], e_sem.at[6 + y], e_sem.at[9 + y], partner) for y in range(3)]

    def swap_start():
        for copy in swaps:
            copy.start()

    def small_start():
        glocal.wait()
        gwait(ahead(at, "x", -1), at["z"], 0)
        gwait(ahead(at, "x", 1), at["z"], 1)
        fwd = gbuf.at[at["z"], ahead(at, "x", -1)]
        gpush(fwd, fwd, 2, xr)

    def small_next():
        gwait(ahead(at, "x", 2), at["z"], 2)
        gpush(gbuf.at[at["z"]], gbuf.at[at["z"]], 3, zo)

    def attn_weights():
        ref = gbuf.at[1 - at["z"]]
        remote(ref, ref, g_send.at[0], g_recv.at[11], partner).wait_recv()
        for copy in swaps:
            copy.wait()
        base = at["c"] * 6
        copies = []
        for y in range(3):
            copies.append(pltpu.make_async_copy(buf.at[y, 0:2], w.at[pl.ds(base + 2 * y, 2)], w_sem.at[y]))
            copies.append(pltpu.make_async_copy(other.at[y], w.at[pl.ds(6 - base + 2 * y, 2)], w_sem.at[3 + y]))
        for copy in copies:
            copy.start()
        spread_gains(gbuf, gain_d, gain_h)
        tok_local.wait()
        ref = tok_out.at[1 - at["t"]]
        remote(ref, ref, e_sem.at[2], e_sem.at[3], partner).wait_recv()
        attn_in[...] = normed(tok_out[...].reshape(attn_in.shape).astype(f32), gain_d[0:1, :])[0].astype(bf16)
        for copy in copies:
            copy.wait()

    pieces = [swap_start, small_start, small_next, attn_weights]
    pieces += attn_forward(at, attn_in, w, cos_ref, sin_ref, allowed_ref, q_raw, k_raw, value, q_rot, k_rot, soft, context, part, gain_h)

    def pair_start():
        far = pl.ds(pl.multiple_of((1 - at["t"]) * 128, 128), 128)
        pstage[...] = part[far, :].astype(bf16)
        pair_copy.start()

    def pair_end():
        near = pl.ds(pl.multiple_of(at["t"] * 128, 128), 128)
        pair_copy.wait()
        raw = part[near, :] + pland[...].astype(f32)
        attn_raw[...] = raw
        res = tok_ref[...].astype(f32) + normed(raw, gain_d[1:2, :])[0]
        residual[...] = res
        ffn_in[...] = normed(res, gain_d[2:3, :])[0].astype(bf16)

    pieces += [pair_start, pair_end]
    for event in order_gather(CLASSES, ATTN_CLASSES, (0.0, 0.0, 3.0, 6.0, 9.0, 12.0, 15.0, 18.0, 20.0, 33.0)):
        if len(event) == 1:
            pieces[event[0]]()
            continue
        k, ph, st = event
        i0, i1, order = CLASSES[k]
        if st == 1:
            await_step(k, ph, 0)
        elif ph > 0:
            await_step(k, ph - 1, 0 if order[ph - 1] == "z" else 1)
        if ph == 3:
            continue
        dim, done = order[ph], order[:ph]
        if ph > 0 and not local_waited:
            local.wait()
            local_waited.append(1)

        def mine_part(lo, hi):
            if ph == 0:
                return own.at[lo:hi]
            return part_of(buf, at, done, dim, at[dim], lo, hi)

        target = part_of(buf, at, done, dim, at[dim], i0, i1)
        if dim == "z":
            push(mine_part(i0, i1), target, k, ph, 0, zo)
            continue
        right, left = device(at, **{dim: ahead(at, dim, 1)}), device(at, **{dim: ahead(at, dim, -1)})
        if st == 0:
            push(mine_part(i0, i1), target, k, ph, 0, right)
            push(mine_part(i0, i1), target, k, ph, 1, left)
        else:
            a = part_of(buf, at, done, dim, ahead(at, dim, -1), i0, i1, 0)
            b = part_of(buf, at, done, dim, ahead(at, dim, 1), i0, i1, 1)
            push(a, a, k, ph, 2, right)
            push(b, b, k, ph, 3, left)
    for copy in pending:
        copy.wait_send()
    tok.wait_send()


def gather_all(w, gains, tokens, cos, sin, allowed):
    n = len(CLASSES)
    dma = pltpu.SemaphoreType.DMA
    half, width = tokens.shape
    rows = 2 * half

    def shape(*dims, kind=f32):
        return jax.ShapeDtypeStruct(dims, kind)

    return pl.pallas_call(
        gather_kernel,
        name="gather_and_attend",
        out_shape=(
            shape(4, 12, 2, 4, ROWS, 128, kind=bf16),
            shape(3, 2, 2, 4, ROWS, 128, kind=bf16),
            shape(rows, width, kind=bf16),
            shape(rows, 512),
            shape(rows, 256),
            shape(rows, 256, kind=bf16),
            shape(rows, 512, kind=bf16),
            shape(rows, 256, kind=bf16),
            shape(2, rows, rows),
            shape(rows, 512, kind=bf16),
            shape(half, width),
            shape(half, width),
            shape(half, width, kind=bf16),
            shape(4, width),
            shape(2, 256),
        ),
        in_specs=[VMEM_SPEC] * 12,
        out_specs=[ANY_SPEC] * 2 + [VMEM_SPEC] * 13,
        scratch_shapes=[
            pltpu.VMEM((8, 12, SHARD, 128), bf16),
            pltpu.VMEM((8, 12, SHARD, 128), bf16),
            pltpu.VMEM((ROWS, 128), f32),
            pltpu.VMEM((12, ROWS, 128), bf16),
            pltpu.VMEM((8, 8, 128), f32),
            pltpu.VMEM((8, 128), f32),
            pltpu.VMEM((2, 4, 8, 128), f32),
            pltpu.VMEM((2, half, width), bf16),
            pltpu.VMEM((12, 2, 4, ROWS, 128), bf16),
            pltpu.VMEM((rows, width), f32),
            pltpu.VMEM((half, width), bf16),
            pltpu.VMEM((half, width), bf16),
            dma((8,)),
            dma((8,)),
            dma((12,)),
            dma((12,)),
            dma((n, 3, 4)),
            dma((n, 3, 4)),
            dma((12,)),
            dma((3,)),
            dma((6,)),
        ],
        compiler_params=pltpu.CompilerParams(collective_id=1, has_side_effects=True, vmem_limit_bytes=VMEM_MOST),
    )(*w, gains, tokens, cos, sin, allowed)


def order_scatter(classes, late, pieces, begin, rate=46e3, hop=2.5):
    free, events, queue = {}, [], []
    for k in range(len(classes)):
        queue.append((begin if k in late else 0.0, k, 0, 0))
    queue += [(t, -1, n, 0) for n, t in enumerate(pieces)]
    while queue:
        queue.sort()
        ready, k, ph, st = queue.pop(0)
        if k < 0:
            events.append((ph,))
            continue
        i0, i1, order = classes[k]
        events.append((k, ph, st))
        if ph == len(order):
            continue
        dim, done = order[2 - ph], order[: 2 - ph]
        size = size_of(done, i1 - i0)
        if dim == "z":
            ways, moved, waited, follow = ("z+",), size, size, (k, ph + 1, 0)
        elif st == 0:
            ways, moved, waited, follow = (dim + "+", dim + "-"), size, size / 2, (k, ph, 1)
        else:
            ways, moved, waited, follow = (dim + "+", dim + "-"), size / 2, size / 2, (k, ph + 1, 0)
        end = 0.0
        for way in ways:
            first = max(ready, free.get(way, 0.0))
            free[way] = first + moved / rate
            end = max(end, first + waited / rate)
        queue.append((end + hop, *follow))
    return events


def recv_shape(done, n, rows):
    return (*((4,) if "y" in done else ()), n, *((2,) if "z" in done else ()), *((4,) if "x" in done else ()), rows, 128)


def scatter_shapes():
    shapes = []
    for i0, i1, order in CLASSES:
        for ph in range(3):
            dim, done = order[2 - ph], order[: 2 - ph]
            for side in (None,) if dim == "z" else (0, 1):
                (lo, hi), rows = side_of(i0, i1, side)
                one = recv_shape(done, hi - lo, rows[1] - rows[0])
                shapes.append(one if side is None else (3, *one))
    return shapes


def combine(target, refs):
    shape = target.shape[:-2]

    @pl.loop(0, math.prod(shape))
    def _(n):
        index, rest = [], n
        for size in reversed(shape):
            index.insert(0, lax.rem(rest, size))
            rest = rest // size
        value = refs[0][tuple(index)].astype(f32)
        for ref in refs[1:]:
            value = value + ref[tuple(index)].astype(f32)
        target[tuple(index)] = value.astype(bf16)


def add_into(target, refs):
    combine(target, [target, *refs])


def rope_back(grad, cos, sin):
    return grad * cos - half_turn(grad * sin)


def scatter_kernel(
    ffn, buf, other, attn_in, q_raw, k_raw, value, q_rot, k_rot, soft, context, attn_raw, residual,
    d_ffn, cot, tok, gain_d, gain_h, gpp, cos, sin,
    q_out, k_out, v_out, o_out, g_out, u_out, d_out, gains_out, tok_out,
    acc, pair, own32, send, got, gacc, grecv, ggot, kv, kvr, gfin, gfinal, gother,
    w, ag, dfull, dctx, dq, dk, dv, part, pstage, pland, gsmall, gheads, *rest,
):
    lands = rest[:-10]
    s_sem, r_sem, a_send, a_recv, g_send, g_recv, e_sem, l_sem, f_sem, w_sem = rest[-10:]
    at = coords()
    group = group_peers(at)
    partner = device(at, c=1 - at["c"])
    mirror = device(at, t=1 - at["t"])
    ring = [device(at, x=ahead(at, "x", 1)), device(at, x=ahead(at, "x", -1)), device(at, z=1 - at["z"])]
    ring.append(device(at, x=ahead(at, "x", 2)))
    loads = {}
    for k, (i0, i1, order) in enumerate(CLASSES):
        loads[k] = []
        for y in range(4):
            if y == 3 or k not in ATTN_CLASSES:
                b = 30 + i0 if y == 3 else 10 * y + i0 - 2
                loads[k].append(pltpu.make_async_copy(ffn.at[b : b + i1 - i0], acc.at[y, i0:i1], f_sem.at[k, y]))
    for k in (*range(2, len(CLASSES)), 0, 1):
        for copy in loads[k]:
            copy.start()
    near = pl.ds(pl.multiple_of(at["t"] * 128, 128), 128)
    far = pl.ds(pl.multiple_of((1 - at["t"]) * 128, 128), 128)
    back, gsmall[2:3, :] = norm_back(residual[...], gain_d[2:3, :], d_ffn[...])
    d_res = cot[...].astype(f32) + back
    tok_out[...] = d_res
    back, gsmall[1:2, :] = norm_back(attn_raw[...], gain_d[1:2, :], d_res)
    dfull[near, :] = back.astype(bf16)
    gsmall[3:4, :] = gpp[...]
    base = at["c"] * 6
    wloads = []
    for y in range(3):
        wloads.append(pltpu.make_async_copy(buf.at[y, 0:2], w.at[pl.ds(base + 2 * y, 2)], w_sem.at[y]))
        wloads.append(pltpu.make_async_copy(other.at[y], w.at[pl.ds(6 - base + 2 * y, 2)], w_sem.at[3 + y]))
    for copy in wloads:
        copy.start()
    enter([device(p) for p in group] + ring + [mirror])
    pending = []

    def push(src, dst, send_sem, recv_sem, to):
        copy = remote(src, dst, send_sem, recv_sem, to)
        copy.start()
        pending.append(copy)

    def await_ref(ref, sem):
        remote(ref, ref, s_sem.at[0, 0, 0], sem, partner).wait_recv()

    zo = device(at, z=1 - at["z"])
    push(dfull.at[near, :], dfull.at[near, :], e_sem.at[6], e_sem.at[7], mirror)
    swap = remote(ag.at[pl.ds(6 - base, 6)], pair, e_sem.at[0], e_sem.at[1], partner)
    pair_copy = remote(pstage, pland, e_sem.at[8], e_sem.at[9], mirror)

    def to_blocks(grad, first):
        grad = grad.astype(bf16)
        for n in range(grad.shape[1] // 128):
            ag[first + n] = grad[:, 128 * n : 128 * n + 128].reshape(2, 4, ROWS, 128)

    def contexts():
        await_ref(dfull.at[far, :], e_sem.at[7])
        for copy in wloads:
            copy.wait()
        dctx[...] = jnp.dot(dfull[...], blocks_of(w, 8, 4), preferred_element_type=f32).astype(bf16)

    def heads():
        dk_rot = jnp.zeros((256, 256), f32)
        d_value = jnp.zeros((256, 256), f32)
        gq = jnp.zeros((1, 256), f32)
        for h in range(2):
            lanes = slice(256 * h, 256 * h + 256)
            d_prob = last_dot(dctx[:, lanes], value[...])
            full = soft[h]
            delta = jnp.sum(full * d_prob, axis=-1, keepdims=True)
            d_score = full * (d_prob - delta) * (256.0 ** -0.5)
            score_b = d_score.astype(bf16)
            dq_norm = rope_back(jnp.dot(score_b, k_rot[...], preferred_element_type=f32), cos[...], sin[...])
            back, gain_part = norm_back(q_raw[:, lanes], gain_h[0:1, :], dq_norm)
            dq[:, lanes] = back.astype(bf16)
            gq = gq + gain_part
            dk_rot = dk_rot + jnp.dot(score_b.T, q_rot[:, lanes], preferred_element_type=f32)
            d_value = d_value + jnp.dot(full.astype(bf16).T, dctx[:, lanes], preferred_element_type=f32)
        back, gk = norm_back(k_raw[...], gain_h[1:2, :], rope_back(dk_rot, cos[...], sin[...]))
        dk[...] = back.astype(bf16)
        dv[...] = d_value.astype(bf16)
        gheads[0:1, :] = gq
        gheads[1:2, :] = gk

    def inputs():
        part[...] = (
            last_dot(dq[...], blocks_of(w, 0, 4))
            + last_dot(dk[...], blocks_of(w, 4, 2))
            + last_dot(dv[...], blocks_of(w, 6, 2))
        )
        pstage[...] = part[far, :].astype(bf16)
        pair_copy.start()

    def weight_grads():
        left = attn_in[...].T
        to_blocks(jnp.dot(left, dq[...], preferred_element_type=f32), 0)
        to_blocks(jnp.dot(left, dk[...], preferred_element_type=f32), 4)
        to_blocks(jnp.dot(left, dv[...], preferred_element_type=f32), 6)

    def out_grads():
        to_blocks(jnp.dot(dfull[...].T, context[...], preferred_element_type=f32), 8)
        swap.start()

    def finish():
        pair_copy.wait()
        d_in = part[near, :] + pland[...].astype(f32)
        back, gsmall[0:1, :] = norm_back(tok[...].astype(f32), gain_d[0:1, :], d_in)
        tok_out[...] = tok_out[...] + back
        folded = fold_gains([gsmall[n : n + 1, :] for n in range(4)], [gheads[n : n + 1, :] for n in range(2)])
        gacc[...] = folded.reshape(2, 4, 8, 128)
        push(gacc.at[1 - at["z"]], grecv.at[0:4], g_send.at[8], g_recv.at[8], zo)

    def merge():
        swap.wait()
        for y in range(3):
            combine(acc.at[y, 0:2], [ag.at[pl.ds(base + 2 * y, 2)], pair.at[2 * y : 2 * y + 2]])

    def small_x():
        await_ref(grecv.at[0:4], g_recv.at[8])
        gacc[at["z"]] = gacc[at["z"]] + grecv[0:4]
        for n in range(1, 4):
            xx = ahead(at, "x", n)
            push(gacc.at[at["z"], xx], grecv.at[4 + n], g_send.at[8 + n], g_recv.at[8 + n], device(at, x=xx))

    pieces = [contexts, heads, weight_grads, out_grads, inputs, merge, finish, small_x]
    times = (11.0, 14.0, 18.0, 21.0, 23.0, 26.0, 37.0, 41.0)
    slots, position = {}, 0
    for k, (i0, i1, order) in enumerate(CLASSES):
        for ph in range(3):
            count = 1 if order[2 - ph] == "z" else 2
            slots[k, ph] = lands[position : position + count]
            position += count

    for event in order_scatter(CLASSES, ATTN_CLASSES, times, 26.1):
        if len(event) == 1:
            pieces[event[0]]()
            continue
        k, ph, st = event
        i0, i1, order = CLASSES[k]
        if st == 0 and ph == 0:
            for copy in loads[k]:
                copy.wait()
        if st == 0 and ph > 0:
            dim, done = order[3 - ph], order[: 3 - ph]
            if dim == "z":
                (land,) = slots[k, ph - 1]
                await_ref(land, r_sem.at[k, ph - 1, 0])
                add_into(part_of(acc, at, done, "z", at["z"], i0, i1), [land])
            else:
                for side, land in enumerate(slots[k, ph - 1]):
                    await_ref(land.at[1], r_sem.at[k, ph - 1, 3 * side + 1])
                    await_ref(land.at[2], r_sem.at[k, ph - 1, 3 * side + 2])
                    add_into(part_of(acc, at, done, dim, at[dim], i0, i1, side), [land.at[1], land.at[2]])
        if ph == 3:
            continue
        dim, done = order[2 - ph], order[: 2 - ph]
        if dim == "z":
            (land,) = slots[k, ph]
            push(part_of(acc, at, done, "z", 1 - at["z"], i0, i1), land, s_sem.at[k, ph, 0], r_sem.at[k, ph, 0], zo)
            continue
        right, left = device(at, **{dim: ahead(at, dim, 1)}), device(at, **{dim: ahead(at, dim, -1)})
        low, high = slots[k, ph]
        p1, m1, p2 = ahead(at, dim, 1), ahead(at, dim, -1), ahead(at, dim, 2)

        def move(index, side, n, to):
            src = part_of(acc, at, done, dim, index, i0, i1, side)
            push(src, slots[k, ph][side].at[n], s_sem.at[k, ph, 3 * side + n], r_sem.at[k, ph, 3 * side + n], to)

        if st == 0:
            move(p2, 0, 0, right)
            move(p2, 1, 0, left)
            move(p1, 1, 1, right)
            move(m1, 0, 2, left)
        else:
            await_ref(low.at[0], r_sem.at[k, ph, 0])
            add_into(part_of(acc, at, done, dim, p1, i0, i1, 0), [low.at[0]])
            move(p1, 0, 1, right)
            await_ref(high.at[0], r_sem.at[k, ph, 3])
            add_into(part_of(acc, at, done, dim, m1, i0, i1, 1), [high.at[0]])
            move(m1, 1, 2, left)

    mine = at["y"] * 2 + at["c"]
    me = slot_of(at)

    @pl.loop(0, 12)
    def _(i):
        own32[...] = acc[at["y"], i, at["z"], at["x"]].astype(f32)
        for s in range(8):
            send[s, i] = own32[SHARD * s : SHARD * (s + 1), :].astype(bf16)

    for n, p in enumerate(group):
        s = p["y"] * 2 + p["c"]
        push(send.at[s], got.at[me], a_send.at[n], a_recv.at[me], device(p))
    here = pltpu.make_async_copy(send.at[mine], got.at[me], l_sem.at[0])
    here.start()
    gsum = gacc[at["z"], at["x"]]
    for n in range(1, 4):
        await_ref(grecv.at[4 + n], g_recv.at[8 + n])
        gsum = gsum + grecv[4 + n]
    gfin[...] = gsum
    for n, p in enumerate(group):
        push(gfin, ggot.at[mine], g_send.at[n], g_recv.at[mine], device(p))
    here.wait()
    for p in group:
        ref = got.at[slot_of(p)]
        await_ref(ref, a_recv.at[slot_of(p)])
    ggot[mine] = gsum
    for p in group:
        s = p["y"] * 2 + p["c"]
        await_ref(ggot.at[s], g_recv.at[s])
    total = ggot[0]
    for s in range(1, 8):
        total = total + ggot[s]
    gfinal[...] = total
    outs = {"q": q_out, "o": o_out, "g": g_out, "u": u_out, "d": d_out}
    later = []
    for k, blocks in enumerate(block_sources()):
        for pos, source in enumerate(blocks):
            if source is None:
                continue
            y, i = divmod(pos, 12)
            name, j = source
            if name in "kv":
                j += 2 if name == "v" else 0
                kv[:, j * 128 : (j + 1) * 128] = got[k * 4 + y, i].astype(f32)
            else:
                later.append((name, j, k * 4 + y, i))
    push(kv, kvr, e_sem.at[2], e_sem.at[3], mirror)
    push(gfinal, gother, e_sem.at[4], e_sem.at[5], mirror)
    for name, j, s, i in later:
        outs[name][:, j * 128 : (j + 1) * 128] = got[s, i].astype(f32)
    await_ref(kvr, e_sem.at[3])
    await_ref(gother, e_sem.at[5])
    k_out[...] = kv[:, 0:256] + kvr[:, 0:256]
    v_out[...] = kv[:, 256:512] + kvr[:, 256:512]
    gains_out[...] = gfinal[...] + gother[...]
    for copy in pending:
        copy.wait_send()


def scatter_all(*operands):
    n = len(CLASSES)
    dma = pltpu.SemaphoreType.DMA
    widths = (512, 256, 256, 512, 3456, 3456, 3456)
    out = [jax.ShapeDtypeStruct((SHARD, w), f32) for w in widths]
    out += [jax.ShapeDtypeStruct((8, 128), f32), jax.ShapeDtypeStruct((128, 8 * ROWS), f32)]
    return pl.pallas_call(
        scatter_kernel,
        name="attend_back_and_scatter",
        out_shape=tuple(out),
        in_specs=[ANY_SPEC] * 3 + [VMEM_SPEC] * 18,
        out_specs=[VMEM_SPEC] * 9,
        scratch_shapes=[
            pltpu.VMEM((4, 12, 2, 4, ROWS, 128), bf16),
            pltpu.VMEM((6, 2, 4, ROWS, 128), bf16),
            pltpu.VMEM((ROWS, 128), f32),
            pltpu.VMEM((8, 12, SHARD, 128), bf16),
            pltpu.VMEM((8, 12, SHARD, 128), bf16),
            pltpu.VMEM((2, 4, 8, 128), f32),
            pltpu.VMEM((8, 8, 128), f32),
            pltpu.VMEM((8, 8, 128), f32),
            pltpu.VMEM((SHARD, 512), f32),
            pltpu.VMEM((SHARD, 512), f32),
            pltpu.VMEM((8, 128), f32),
            pltpu.VMEM((8, 128), f32),
            pltpu.VMEM((8, 128), f32),
            pltpu.VMEM((12, 2, 4, ROWS, 128), bf16),
            pltpu.VMEM((12, 2, 4, ROWS, 128), bf16),
            pltpu.VMEM((256, 8 * ROWS), bf16),
            pltpu.VMEM((256, 512), bf16),
            pltpu.VMEM((256, 512), bf16),
            pltpu.VMEM((256, 256), bf16),
            pltpu.VMEM((256, 256), bf16),
            pltpu.VMEM((256, 8 * ROWS), f32),
            pltpu.VMEM((128, 8 * ROWS), bf16),
            pltpu.VMEM((128, 8 * ROWS), bf16),
            pltpu.VMEM((4, 8 * ROWS), f32),
            pltpu.VMEM((2, 256), f32),
            *[pltpu.VMEM(s, bf16) for s in scatter_shapes()],
            dma((n, 3, 6)),
            dma((n, 3, 6)),
            dma((8,)),
            dma((8,)),
            dma((12,)),
            dma((12,)),
            dma((10,)),
            dma((6,)),
            dma((n, 4)),
            dma((6,)),
        ],
        compiler_params=pltpu.CompilerParams(collective_id=2, has_side_effects=True, vmem_limit_bytes=VMEM_MOST),
    )(*operands)


def ffn_kernel(
    x_in, res, cot, gain, buf,
    out, d_in, gpp, grads,
    w, dw, xs, ds, xt, dt, gates, ups, part, land_a, land_b, zstage, zland_a, zland_b,
    w_sem, dw_sem, s_sem, r_sem,
):
    at = coords()
    mirror = device(at, t=1 - at["t"])
    partner = device(at, c=1 - at["c"])
    pairs = 7
    loads = []
    for j in range(pairs):
        for n in range(3):
            lo = n * 14 + 2 * j
            copy = pltpu.make_async_copy(buf.at[place(lo) : place(lo) + 2], w.at[lo : lo + 2], w_sem.at[j, n])
            copy.start()

    def rows(c, t, n=1):
        return pl.ds(pl.multiple_of((c * 2 + t) * 128, 128), 128 * n)

    enter([mirror, partner])
    c, t = at["c"], at["t"]

    def gather(e, full):
        view = lambda cc, tt: full.at[rows(cc, tt), :]
        a = remote(view(c, t), view(c, t), s_sem.at[e, 0], r_sem.at[e, 0], mirror)
        b = remote(view(c, t), view(c, t), s_sem.at[e, 1], r_sem.at[e, 1], partner)
        a.start()
        b.start()
        ref = view(c, 1 - t)
        remote(ref, ref, s_sem.at[e, 0], r_sem.at[e, 0], mirror).wait_recv()
        f = remote(ref, ref, s_sem.at[e, 2], r_sem.at[e, 2], partner)
        f.start()
        one, two = view(1 - c, t), view(1 - c, 1 - t)
        remote(one, one, s_sem.at[e, 0], r_sem.at[e, 1], mirror).wait_recv()
        remote(two, two, s_sem.at[e, 0], r_sem.at[e, 2], mirror).wait_recv()
        for copy in (a, b, f):
            copy.wait_send()

    def reduce(e, land, zland):
        a = remote(part.at[rows(1 - c, 0, 2), :], land, s_sem.at[e, 0], r_sem.at[e, 0], partner)
        a.start()
        a.wait()
        far = pl.ds(pl.multiple_of((1 - t) * 128, 128), 128)
        near = pl.ds(pl.multiple_of(t * 128, 128), 128)
        zstage[...] = (part[rows(c, 1 - t), :] + land[far, :]).astype(bf16)
        b = remote(zstage, zland, s_sem.at[e, 1], r_sem.at[e, 1], mirror)
        b.start()
        kept = part[rows(c, t), :] + land[near, :]
        b.wait()
        return kept + zland[...].astype(f32)

    xs[rows(c, t), :] = x_in[...]
    gather(0, xs)
    part[...] = jnp.zeros_like(part)

    def weights(j, n):
        return jnp.concatenate([w[n * 14 + 2 * j], w[n * 14 + 2 * j + 1]], axis=1)

    def rows_dot(a, b):
        return lax.dot_general(a, b, (((1,), (1,)), ((), ())), preferred_element_type=f32)

    @pl.loop(0, pairs)
    def _(j):
        lanes = pl.ds(pl.multiple_of(j * 256, 256), 256)
        for n in range(3):
            pltpu.make_async_copy(buf.at[0:2], w.at[0:2], w_sem.at[j, n]).wait()
        gate = jnp.dot(xs[...], weights(j, 0), preferred_element_type=f32)
        up = jnp.dot(xs[...], weights(j, 1), preferred_element_type=f32)
        gates[:, lanes] = gate
        ups[:, lanes] = up
        act = 0.5 * gate * (1.0 + jnp.tanh(gelu_scale * (gate + gelu_cube * gate * gate * gate)))
        hidden = (act * up).astype(bf16)
        part[...] += rows_dot(hidden, weights(j, 2))

    raw = reduce(1, land_a, zland_a)
    width = raw.shape[1]
    inverse = lax.rsqrt(jnp.sum(raw * raw, axis=-1, keepdims=True) * (1.0 / width) + eps)
    gained = 1.0 + gain[...]
    out[...] = (res[...] + raw * inverse * gained).astype(bf16)
    g = cot[...].astype(f32)
    scaled = g * gained
    mean = jnp.sum(scaled * raw, axis=-1, keepdims=True) * (1.0 / width)
    ds[rows(c, t), :] = (inverse * scaled - raw * inverse * inverse * inverse * mean).astype(bf16)
    gpp[...] = jnp.sum(g * raw * inverse, axis=0, keepdims=True)
    gather(2, ds)
    xt[...] = xs[...].T
    dt[...] = ds[...].T
    part[...] = jnp.zeros_like(part)

    @pl.loop(0, pairs)
    def _(j):
        lanes = pl.ds(pl.multiple_of(j * 256, 256), 256)
        gate, up = gates[:, lanes], ups[:, lanes]
        d_hidden = jnp.dot(ds[...], weights(j, 2), preferred_element_type=f32)
        tanh = jnp.tanh(gelu_scale * (gate + gelu_cube * gate * gate * gate))
        act = 0.5 * gate * (1.0 + tanh)
        slope = 0.5 * (1.0 + tanh) + 0.5 * gate * (1.0 - tanh * tanh) * gelu_scale * (
            1.0 + 3.0 * gelu_cube * gate * gate
        )
        hidden = (act * up).astype(bf16)
        d_gate = (d_hidden * up * slope).astype(bf16)
        d_up = (d_hidden * act).astype(bf16)
        part[...] += rows_dot(d_gate, weights(j, 0)) + rows_dot(d_up, weights(j, 1))
        for n, (left, right) in enumerate(((xt, d_gate), (xt, d_up), (dt, hidden))):
            grad = jnp.dot(left[...], right, preferred_element_type=f32).astype(bf16)
            lo = n * 14 + 2 * j
            dw[lo] = grad[:, :128]
            dw[lo + 1] = grad[:, 128:]
            pltpu.make_async_copy(dw.at[pl.ds(lo, 2)], grads.at[pl.ds(lo, 2)], dw_sem.at[j, n]).start()

    d_in[...] = reduce(3, land_b, zland_b)
    for j in range(pairs):
        for n in range(3):
            lo = n * 14 + 2 * j
            pltpu.make_async_copy(dw.at[lo : lo + 2], grads.at[lo : lo + 2], dw_sem.at[j, n]).wait()


def ffn_all(x_in, res, cot, gain, buf):
    dma = pltpu.SemaphoreType.DMA
    tokens, width = x_in.shape
    return pl.pallas_call(
        ffn_kernel,
        name="ffn_layer",
        out_shape=(
            jax.ShapeDtypeStruct((tokens, width), bf16),
            jax.ShapeDtypeStruct((tokens, width), f32),
            jax.ShapeDtypeStruct((1, width), f32),
            jax.ShapeDtypeStruct((42, width, 128), bf16),
        ),
        in_specs=[VMEM_SPEC] * 4 + [ANY_SPEC],
        out_specs=[VMEM_SPEC] * 3 + [ANY_SPEC],
        scratch_shapes=[
            pltpu.VMEM((42, width, 128), bf16),
            pltpu.VMEM((42, width, 128), bf16),
            pltpu.VMEM((512, width), bf16),
            pltpu.VMEM((512, width), bf16),
            pltpu.VMEM((width, 512), bf16),
            pltpu.VMEM((width, 512), bf16),
            pltpu.VMEM((512, 1792), f32),
            pltpu.VMEM((512, 1792), f32),
            pltpu.VMEM((512, width), f32),
            pltpu.VMEM((256, width), f32),
            pltpu.VMEM((256, width), f32),
            pltpu.VMEM((128, width), bf16),
            pltpu.VMEM((128, width), bf16),
            pltpu.VMEM((128, width), bf16),
            dma((7, 3)),
            dma((7, 3)),
            dma((4, 3)),
            dma((4, 3)),
        ],
        compiler_params=pltpu.CompilerParams(collective_id=3, has_side_effects=True, vmem_limit_bytes=VMEM_MOST),
    )(x_in, res, cot, gain, buf)


def local(
    tokens,
    segment_ids,
    w_query,
    w_key,
    w_value,
    w_out,
    gain_query,
    gain_key,
    gain_pre_attn,
    gain_post_attn,
    w_gate,
    w_up,
    w_down,
    gain_pre_ffn,
    gain_post_ffn,
    cotangent,
):
    my_dp = lax.axis_index("dp")
    packed = jnp.concatenate(
        [gain_pre_attn, gain_post_attn, gain_pre_ffn, gain_post_ffn, gain_query, gain_key]
    ).astype(f32)
    packed = jnp.broadcast_to(jnp.pad(packed, (0, 48))[None], (8, 128))
    width = tokens.shape[1]
    segment_row = segment_ids[0]
    cos, sin = rope_tables(positions_of(segment_row), 256)
    allowed = build_allowed(segment_row).astype(f32)
    (
        buf, other, attn_in, q_raw, k_raw, value, q_rot, k_rot, soft, context, attn_raw, residual, ffn_in, gain_d, gain_h,
    ) = gather_all((w_query, w_key, w_value, w_out, w_gate, w_up, w_down), packed, tokens, cos, sin, allowed)
    output, d_ffn, gpp, ffn_grads = ffn_all(ffn_in, residual, cotangent, gain_d[3:4], buf.reshape(48, width, 128))
    sums = scatter_all(
        ffn_grads.reshape(42, 2, 4, ROWS, 128), buf, other, attn_in, q_raw, k_raw, value, q_rot, k_rot, soft, context,
        attn_raw, residual, d_ffn, cotangent, tokens, gain_d, gain_h, gpp, cos, sin,
    )
    s_query, s_key, s_value, s_out, s_gate, s_up, s_down, s_gains, grad_tokens = sums
    s_gains = lax.dynamic_index_in_dim(s_gains, lax.rem(my_dp, 8), 0, keepdims=False)
    s_pa, s_po, s_pf, s_pp = [s_gains[18 * n : 18 * n + 18] for n in range(4)]
    return (
        output, grad_tokens, s_query, s_key, s_value, s_out, s_gains[72:76], s_gains[76:80],
        s_pa, s_po, s_gate, s_up, s_down, s_pf, s_pp,
    )


def solution(mesh):
    return jax.shard_map(
        local,
        mesh=mesh,
        in_specs=(
            P(("dp", "tensor"), None),
            P("dp", None),
            P("dp", "tensor"),
            P("dp", None),
            P("dp", None),
            P("dp", "tensor"),
            P("dp"),
            P("dp"),
            P("dp"),
            P("dp"),
            P("dp", "tensor"),
            P("dp", "tensor"),
            P("dp", "tensor"),
            P("dp"),
            P("dp"),
            P(("dp", "tensor"), None),
        ),
        out_specs=(
            P(("dp", "tensor"), None),
            P(("dp", "tensor"), None),
            P("dp", "tensor"),
            P("dp", None),
            P("dp", None),
            P("dp", "tensor"),
            P("dp"),
            P("dp"),
            P("dp"),
            P("dp"),
            P("dp", "tensor"),
            P("dp", "tensor"),
            P("dp", "tensor"),
            P("dp"),
            P("dp"),
        ),
        check_vma=False,
    )
```

```python
import functools
import math

import jax
import jax.numpy as jnp
from jax import lax
from jax.experimental import pallas as pl
from jax.experimental.pallas import tpu as pltpu
from jax.sharding import PartitionSpec as P

eps = 1e-06
gelu_scale = 0.7978845608028654
gelu_cube = 0.044715


f32 = jnp.float32
bf16 = jnp.bfloat16
MESH = pl.DeviceIdType.MESH
ROWS = 144
SHARD = 18
VMEM_SPEC = pl.BlockSpec(memory_space=pltpu.VMEM)
ANY_SPEC = pl.BlockSpec(memory_space=pl.ANY)
VMEM_MOST = 66_000_000

CLASSES = (
    (0, 1, "zxy"),
    (1, 2, "zyx"),
    (2, 4, "zxy"),
    (4, 6, "zyx"),
    (6, 8, "zxy"),
    (8, 10, "zyx"),
    (10, 11, "xyz"),
    (11, 12, "yxz"),
)
ATTN_CLASSES = (0, 1)
ROW_CUT = 80


def place(block):
    return block // 10 * 12 + 2 + block % 10 if block < 30 else 6 + block


def attn_place(block):
    return block // 2 * 12 + block % 2


def coords():
    dp, t = lax.axis_index("dp"), lax.axis_index("tensor")
    return {"c": lax.rem(dp, 2), "y": lax.rem(dp // 2, 4), "x": lax.rem(dp // 8, 4), "z": dp // 32, "t": t}


def device(at, **change):
    p = {**at, **change}
    return (((p["z"] * 4 + p["x"]) * 4 + p["y"]) * 2 + p["c"], p["t"])


def ahead(at, dim, by):
    size = 2 if dim == "z" else 4
    return lax.rem(at[dim] + by + size, size)


def block_sources():
    attn = [("q", j) for j in range(4)] + [("k", j) for j in range(2)]
    attn_two = [("v", j) for j in range(2)] + [("o", j) for j in range(4)]
    ffn = [[(n, j) for n in "gud" for j in range(14)], [(n, j + 14) if j < 13 else None for n in "gud" for j in range(14)]]
    cores = []
    for small, large in ((attn, ffn[0]), (attn_two, ffn[1])):
        spots = [None] * 48
        for n, source in enumerate(small):
            spots[attn_place(n)] = source
        for n, source in enumerate(large):
            spots[place(n)] = source
        cores.append(spots)
    return cores


def enter(peers):
    barrier = pltpu.get_barrier_semaphore()
    for peer in peers:
        pl.semaphore_signal(barrier, inc=1, device_id=peer, device_id_type=MESH)
    pl.semaphore_wait(barrier, len(peers))


def remote(src, dst, send, recv, to):
    return pltpu.make_async_remote_copy(
        src_ref=src, dst_ref=dst, send_sem=send, recv_sem=recv, device_id=to, device_id_type=MESH
    )


def group_peers(at):
    peers = []
    for dy in range(4):
        for dc in range(2):
            if dy or dc:
                peers.append({**at, "y": ahead(at, "y", dy), "c": lax.rem(at["c"] + dc, 2)})
    return peers


def slot_of(p):
    return p["c"] * 4 + p["y"]


def part_of(buf, at, done, dim, index, i0, i1, side=None):
    pick = {d: (slice(None) if d in done else at[d]) for d in "zxy"}
    if dim is not None:
        pick[dim] = index
    (lo, hi), rows = side_of(i0, i1, side)
    return buf.at[pick["y"], lo:hi, pick["z"], pick["x"], rows[0] : rows[1]]


def side_of(i0, i1, side):
    n = i1 - i0
    if side is None:
        return (i0, i1), (0, ROWS)
    if n % 2 == 0:
        mid = i0 + n // 2
        return ((i0, mid), (mid, i1))[side], (0, ROWS)
    return (i0, i1), ((0, ROW_CUT), (ROW_CUT, ROWS))[side]


def size_of(done, n):
    size = n * ROWS * 128 * 2
    for d in done:
        size *= 2 if d == "z" else 4
    return size


def order_gather(classes, early, pieces, rate=46e3, hop=1.6):
    free, events, queue = {}, [], []
    left = len(early)
    for k in range(len(classes)):
        queue.append((0.0, k, 0, 0))
    while queue:
        queue.sort()
        ready, k, ph, st = queue.pop(0)
        if k < 0:
            events.append((ph,))
            continue
        i0, i1, order = classes[k]
        events.append((k, ph, st))
        if ph == len(order):
            left -= k in early
            if k in early and not left:
                queue += [(ready + t, -1, n, 0) for n, t in enumerate(pieces)]
            continue
        dim, done = order[ph], order[:ph]
        size = size_of(done, i1 - i0)
        if dim == "z":
            ways, moved, follow = ("z+",), size, (k, ph + 1, 0)
        elif st == 0:
            ways, moved, follow = (dim + "+", dim + "-"), size, (k, ph, 1)
        else:
            ways, moved, follow = (dim + "+", dim + "-"), size / 2, (k, ph + 1, 0)
        end = 0.0
        for way in ways:
            free[way] = max(ready, free.get(way, 0.0)) + moved / rate
            end = max(end, free[way])
        queue.append((end + hop, *follow))
    return events


def write_tables(seg_ref, cos_ref, sin_ref, allowed_ref):
    rows = seg_ref.shape[1]
    across = jnp.broadcast_to(seg_ref[...].astype(f32), (rows, rows))
    same = across == across.T
    a = lax.broadcasted_iota(jnp.int32, (rows, rows), 0).astype(f32)
    b = lax.broadcasted_iota(jnp.int32, (rows, rows), 1).astype(f32)
    allowed_ref[...] = jnp.where(same & (b <= a), 1.0, 0.0)
    begin = jnp.min(jnp.where(same, b, float(rows)), axis=1, keepdims=True)
    position = a[:, :128] - begin
    j = lax.broadcasted_iota(jnp.int32, (rows, 128), 1).astype(f32)
    angles = position * jnp.exp(j * (-2.0 * math.log(10000.0) / 256))
    for table, values in ((cos_ref, jnp.cos(angles)), (sin_ref, jnp.sin(angles))):
        table[:, :128] = values
        table[:, 128:] = values


def normed(values, gain):
    inverse = lax.rsqrt(jnp.mean(values * values, axis=-1, keepdims=True) + eps)
    return values * inverse * (1.0 + gain), inverse


def norm_back(values, gain, grad):
    inverse = lax.rsqrt(jnp.mean(values * values, axis=-1, keepdims=True) + eps)
    scaled = grad * (1.0 + gain)
    mean = jnp.mean(scaled * values, axis=-1, keepdims=True)
    back = inverse * scaled - values * inverse * inverse * inverse * mean
    return back, jnp.sum(grad * values * inverse, axis=0, keepdims=True)


def half_turn(values):
    return jnp.concatenate([-values[:, 128:], values[:, :128]], axis=1)


def last_dot(a, b):
    return lax.dot_general(a, b, (((1,), (1,)), ((), ())), preferred_element_type=f32)


def spread_marks(each, offset, width):
    lane = lax.broadcasted_iota(jnp.int32, (128, width), 0)
    entry = lax.broadcasted_iota(jnp.int32, (128, width), 1)
    picks = lane == offset + lax.rem(entry, each)
    dev = lax.broadcasted_iota(jnp.int32, (64, width), 0)
    owns = lax.div(lax.broadcasted_iota(jnp.int32, (64, width), 1), each) == dev
    return picks, owns


def spread_gains(gbuf, gain_d, gain_h):
    tile = gbuf[...].reshape(64, 128).astype(bf16)
    for n in range(4):
        picks, owns = spread_marks(SHARD, SHARD * n, gain_d.shape[1])
        wide = jnp.dot(tile, picks.astype(f32).astype(bf16), preferred_element_type=f32)
        gain_d[n : n + 1, :] = jnp.sum(jnp.where(owns, wide, 0.0), axis=0, keepdims=True)
    for n in range(2):
        picks, owns = spread_marks(4, 4 * SHARD + 4 * n, 256)
        wide = jnp.dot(tile, picks.astype(f32).astype(bf16), preferred_element_type=f32)
        gain_h[n : n + 1, :] = jnp.sum(jnp.where(owns, wide, 0.0), axis=0, keepdims=True)


def fold_gains(grads_d, grads_h):
    total = jnp.zeros((64, 128), f32)
    for n in range(4):
        picks, owns = spread_marks(SHARD, SHARD * n, grads_d[n].shape[1])
        wide = jnp.where(owns, grads_d[n], 0.0)
        total += lax.dot_general(
            wide, picks.astype(f32), (((1,), (1,)), ((), ())),
            precision=lax.Precision.HIGHEST, preferred_element_type=f32,
        )
    for n in range(2):
        picks, owns = spread_marks(4, 4 * SHARD + 4 * n, 256)
        wide = jnp.where(owns, grads_h[n], 0.0)
        total += lax.dot_general(
            wide, picks.astype(f32), (((1,), (1,)), ((), ())),
            precision=lax.Precision.HIGHEST, preferred_element_type=f32,
        )
    return total


def blocks_of(w, first, count):
    width = 8 * ROWS
    return jnp.concatenate([w[first + n].reshape(width, 128) for n in range(count)], axis=1)


def attn_forward(at, attn_in, w, cos, sin, allowed, q_raw, k_raw, value, q_rot, k_rot, soft, context, part, gain_h):
    def queries():
        q_raw[...] = jnp.dot(attn_in[...], blocks_of(w, 0, 4), preferred_element_type=f32)
        for h in range(2):
            lanes = slice(256 * h, 256 * h + 256)
            q = normed(q_raw[:, lanes], gain_h[0:1, :])[0]
            q_rot[:, lanes] = (q * cos[...] + half_turn(q) * sin[...]).astype(bf16)

    def keys():
        key = jnp.dot(attn_in[...], blocks_of(w, 4, 2), preferred_element_type=f32)
        k_raw[...] = key
        key = normed(key, gain_h[1:2, :])[0]
        k_rot[...] = (key * cos[...] + half_turn(key) * sin[...]).astype(bf16)
        value[...] = jnp.dot(attn_in[...], blocks_of(w, 6, 2), preferred_element_type=f32).astype(bf16)

    def heads():
        seen = allowed[...] > 0.0
        for h in range(2):
            lanes = slice(256 * h, 256 * h + 256)
            scores = last_dot(q_rot[:, lanes], k_rot[...]) * (256.0 ** -0.5)
            scores = jnp.where(seen, scores, -jnp.inf)
            top = jnp.max(scores, axis=-1, keepdims=True)
            total = jnp.sum(jnp.exp(scores - top), axis=-1, keepdims=True)
            full = jnp.where(seen, jnp.exp(scores - (top + jnp.log(total))), 0.0)
            soft[h] = full
            context[:, lanes] = jnp.dot(full.astype(bf16), value[...], preferred_element_type=f32).astype(bf16)

    def project():
        part[...] = last_dot(context[...], blocks_of(w, 8, 4))

    return [queries, keys, heads, project]


def gather_kernel(
    q_ref, k_ref, v_ref, o_ref, g_ref, u_ref, d_ref, gains_ref, tok_ref, seg_ref,
    buf, other, attn_in, q_raw, k_raw, value, q_rot, k_rot, soft, context, attn_raw, residual, ffn_full, gain_d, gain_h, cos_ref, sin_ref,
    send, got, own32, own, ggot, gmine, gbuf, tok_out, w, part, pstage, pland, allowed_ref,
    a_send, a_recv, g_send, g_recv, s_sem, r_sem, e_sem, l_sem, w_sem, x_sem,
):
    at = coords()
    refs = {"q": q_ref, "k": k_ref, "v": v_ref, "o": o_ref, "g": g_ref, "u": u_ref, "d": d_ref}
    group = group_peers(at)
    partner = device(at, c=1 - at["c"])
    mirror = device(at, t=1 - at["t"])
    ring = [device(at, x=ahead(at, "x", 1)), device(at, x=ahead(at, "x", -1)), device(at, z=1 - at["z"])]
    for k, blocks in enumerate(block_sources()):
        for pos, source in enumerate(blocks):
            y, i = divmod(pos, 12)
            if source is None:
                send[k * 4 + y, i] = jnp.zeros((SHARD, 128), bf16)
            else:
                name, j = source
                send[k * 4 + y, i] = refs[name][:, j * 128 : (j + 1) * 128]
    row = lax.broadcasted_iota(jnp.int32, (8, 128), 0)
    gmine[...] = jnp.where(row == at["y"] * 2 + at["c"], gains_ref[...], 0.0)
    me = slot_of(at)
    mine = at["y"] * 2 + at["c"]
    enter([device(p) for p in group] + ring + [mirror])
    tok = remote(tok_ref, tok_out.at[at["t"]], e_sem.at[2], e_sem.at[3], mirror)
    tok.start()
    tok_local = pltpu.make_async_copy(tok_ref, tok_out.at[at["t"]], l_sem.at[1])
    tok_local.start()
    first = []
    for n, p in enumerate(group):
        copy = remote(send.at[slot_of(p)], got.at[mine], a_send.at[n], a_recv.at[mine], device(p))
        small = remote(gmine, ggot.at[mine], g_send.at[n], g_recv.at[mine], device(p))
        copy.start()
        small.start()
        first += [copy, small]
    here = pltpu.make_async_copy(send.at[me], got.at[mine], l_sem.at[0])
    here.start()
    write_tables(seg_ref, cos_ref, sin_ref, allowed_ref)
    here.wait()
    for p in group:
        s = p["y"] * 2 + p["c"]
        remote(send.at[0], got.at[s], a_send.at[0], a_recv.at[s], device(p)).wait_recv()
        remote(gmine, ggot.at[s], g_send.at[0], g_recv.at[s], device(p)).wait_recv()
    ggot[mine] = gmine[...]
    gmine_sum = ggot[0]
    for s in range(1, 8):
        gmine_sum = gmine_sum + ggot[s]

    @pl.loop(0, 12)
    def _(i):
        for s in range(8):
            own32[SHARD * s : SHARD * (s + 1), :] = got[s, i].astype(f32)
        own[i] = own32[...].astype(bf16)

    for copy in first:
        copy.wait_send()
    gmine[...] = gmine_sum
    local = pltpu.make_async_copy(own, part_of(buf, at, "", None, None, 0, 12), l_sem.at[0])
    local.start()
    glocal = pltpu.make_async_copy(gmine, gbuf.at[at["z"], at["x"]], l_sem.at[2])
    glocal.start()
    pending = []

    def incoming(k, ph, st):
        i0, i1, order = CLASSES[k]
        dim, done = order[ph], order[:ph]
        if dim == "z":
            return [(part_of(buf, at, done, "z", 1 - at["z"], i0, i1), r_sem.at[k, ph, 0])]
        left, right = ahead(at, dim, -1), ahead(at, dim, 1)
        if st == 0:
            return [
                (part_of(buf, at, done, dim, left, i0, i1), r_sem.at[k, ph, 0]),
                (part_of(buf, at, done, dim, right, i0, i1), r_sem.at[k, ph, 1]),
            ]
        across = ahead(at, dim, 2)
        return [
            (part_of(buf, at, done, dim, across, i0, i1, 0), r_sem.at[k, ph, 2]),
            (part_of(buf, at, done, dim, across, i0, i1, 1), r_sem.at[k, ph, 3]),
        ]

    def await_step(k, ph, st):
        for ref, sem in incoming(k, ph, st):
            remote(ref, ref, s_sem.at[k, ph, 0], sem, partner).wait_recv()

    local_waited = []

    def push(ref_from, ref_to, k, ph, n, to):
        copy = remote(ref_from, ref_to, s_sem.at[k, ph, n], r_sem.at[k, ph, n], to)
        copy.start()
        pending.append(copy)

    def gpush(src, dst, n, to):
        copy = remote(src, dst, g_send.at[8 + n], g_recv.at[8 + n], to)
        copy.start()
        pending.append(copy)

    xr, xl = device(at, x=ahead(at, "x", 1)), device(at, x=ahead(at, "x", -1))
    zo = device(at, z=1 - at["z"])
    gpush(gmine, gbuf.at[at["z"], at["x"]], 0, xr)
    gpush(gmine, gbuf.at[at["z"], at["x"]], 1, xl)

    def gwait(x, z, n):
        ref = gbuf.at[z, x]
        remote(ref, ref, g_send.at[0], g_recv.at[8 + n], partner).wait_recv()

    pair_copy = remote(pstage, pland, e_sem.at[4], e_sem.at[5], mirror)
    swaps = [remote(buf.at[y, 0:2], other.at[y], e_sem.at[6 + y], e_sem.at[9 + y], partner) for y in range(3)]

    def swap_start():
        for copy in swaps:
            copy.start()

    def small_start():
        glocal.wait()
        gwait(ahead(at, "x", -1), at["z"], 0)
        gwait(ahead(at, "x", 1), at["z"], 1)
        fwd = gbuf.at[at["z"], ahead(at, "x", -1)]
        gpush(fwd, fwd, 2, xr)

    def small_next():
        gwait(ahead(at, "x", 2), at["z"], 2)
        gpush(gbuf.at[at["z"]], gbuf.at[at["z"]], 3, zo)

    def attn_weights():
        ref = gbuf.at[1 - at["z"]]
        remote(ref, ref, g_send.at[0], g_recv.at[11], partner).wait_recv()
        for copy in swaps:
            copy.wait()
        base = at["c"] * 6
        copies = []
        for y in range(3):
            copies.append(pltpu.make_async_copy(buf.at[y, 0:2], w.at[pl.ds(base + 2 * y, 2)], w_sem.at[y]))
            copies.append(pltpu.make_async_copy(other.at[y], w.at[pl.ds(6 - base + 2 * y, 2)], w_sem.at[3 + y]))
        for copy in copies:
            copy.start()
        spread_gains(gbuf, gain_d, gain_h)
        tok_local.wait()
        ref = tok_out.at[1 - at["t"]]
        remote(ref, ref, e_sem.at[2], e_sem.at[3], partner).wait_recv()
        attn_in[...] = normed(tok_out[...].reshape(attn_in.shape).astype(f32), gain_d[0:1, :])[0].astype(bf16)
        for copy in copies:
            copy.wait()

    pieces = [swap_start, small_start, small_next, attn_weights]
    pieces += attn_forward(at, attn_in, w, cos_ref, sin_ref, allowed_ref, q_raw, k_raw, value, q_rot, k_rot, soft, context, part, gain_h)

    def pair_start():
        far = pl.ds(pl.multiple_of((1 - at["t"]) * 128, 128), 128)
        pstage[...] = part[far, :].astype(bf16)
        pair_copy.start()

    def pair_end():
        near = pl.ds(pl.multiple_of(at["t"] * 128, 128), 128)
        pair_copy.wait()
        raw = part[near, :] + pland[...].astype(f32)
        attn_raw[...] = raw
        res = tok_ref[...].astype(f32) + normed(raw, gain_d[1:2, :])[0]
        residual[...] = res
        ffn_full[quarter(at["c"], at["t"]), :] = normed(res, gain_d[2:3, :])[0].astype(bf16)
        for copy in spread[:2]:
            copy.start()

    def pass_on():
        spread[0].wait_recv()
        spread[2].start()

    def quarter(c, t):
        return pl.ds(pl.multiple_of((c * 2 + t) * 128, 128), 128)

    mine_q = ffn_full.at[quarter(at["c"], at["t"]), :]
    far_q = ffn_full.at[quarter(at["c"], 1 - at["t"]), :]
    spread = [
        remote(mine_q, mine_q, x_sem.at[0], x_sem.at[1], mirror),
        remote(mine_q, mine_q, x_sem.at[2], x_sem.at[3], partner),
        remote(far_q, far_q, x_sem.at[4], x_sem.at[5], partner),
    ]
    pieces += [pair_start, pair_end, pass_on]
    for event in order_gather(CLASSES, ATTN_CLASSES, (0.0, 0.0, 3.0, 6.0, 9.0, 12.0, 15.0, 18.0, 20.0, 31.0, 42.0)):
        if len(event) == 1:
            pieces[event[0]]()
            continue
        k, ph, st = event
        i0, i1, order = CLASSES[k]
        if st == 1:
            await_step(k, ph, 0)
        elif ph > 0:
            await_step(k, ph - 1, 0 if order[ph - 1] == "z" else 1)
        if ph == 3:
            continue
        dim, done = order[ph], order[:ph]
        if ph > 0 and not local_waited:
            local.wait()
            local_waited.append(1)

        def mine_part(lo, hi):
            if ph == 0:
                return own.at[lo:hi]
            return part_of(buf, at, done, dim, at[dim], lo, hi)

        target = part_of(buf, at, done, dim, at[dim], i0, i1)
        if dim == "z":
            push(mine_part(i0, i1), target, k, ph, 0, zo)
            continue
        right, left = device(at, **{dim: ahead(at, dim, 1)}), device(at, **{dim: ahead(at, dim, -1)})
        if st == 0:
            push(mine_part(i0, i1), target, k, ph, 0, right)
            push(mine_part(i0, i1), target, k, ph, 1, left)
        else:
            a = part_of(buf, at, done, dim, ahead(at, dim, -1), i0, i1, 0)
            b = part_of(buf, at, done, dim, ahead(at, dim, 1), i0, i1, 1)
            push(a, a, k, ph, 2, right)
            push(b, b, k, ph, 3, left)
    for copy in pending:
        copy.wait_send()
    tok.wait_send()
    spread[0].wait_send()
    spread[1].wait()
    spread[2].wait()


def gather_all(w, gains, tokens, segments):
    n = len(CLASSES)
    dma = pltpu.SemaphoreType.DMA
    half, width = tokens.shape
    rows = 2 * half

    def shape(*dims, kind=f32):
        return jax.ShapeDtypeStruct(dims, kind)

    return pl.pallas_call(
        gather_kernel,
        name="gather_and_attend",
        out_shape=(
            shape(4, 12, 2, 4, ROWS, 128, kind=bf16),
            shape(3, 2, 2, 4, ROWS, 128, kind=bf16),
            shape(rows, width, kind=bf16),
            shape(rows, 512),
            shape(rows, 256),
            shape(rows, 256, kind=bf16),
            shape(rows, 512, kind=bf16),
            shape(rows, 256, kind=bf16),
            shape(2, rows, rows),
            shape(rows, 512, kind=bf16),
            shape(half, width),
            shape(half, width),
            shape(4 * half, width, kind=bf16),
            shape(4, width),
            shape(2, 256),
            shape(rows, 256),
            shape(rows, 256),
        ),
        in_specs=[VMEM_SPEC] * 10,
        out_specs=[ANY_SPEC] * 2 + [VMEM_SPEC] * 15,
        scratch_shapes=[
            pltpu.VMEM((8, 12, SHARD, 128), bf16),
            pltpu.VMEM((8, 12, SHARD, 128), bf16),
            pltpu.VMEM((ROWS, 128), f32),
            pltpu.VMEM((12, ROWS, 128), bf16),
            pltpu.VMEM((8, 8, 128), f32),
            pltpu.VMEM((8, 128), f32),
            pltpu.VMEM((2, 4, 8, 128), f32),
            pltpu.VMEM((2, half, width), bf16),
            pltpu.VMEM((12, 2, 4, ROWS, 128), bf16),
            pltpu.VMEM((rows, width), f32),
            pltpu.VMEM((half, width), bf16),
            pltpu.VMEM((half, width), bf16),
            pltpu.VMEM((rows, rows), f32),
            dma((8,)),
            dma((8,)),
            dma((12,)),
            dma((12,)),
            dma((n, 3, 4)),
            dma((n, 3, 4)),
            dma((12,)),
            dma((3,)),
            dma((6,)),
            dma((6,)),
        ],
        compiler_params=pltpu.CompilerParams(collective_id=1, has_side_effects=True, vmem_limit_bytes=VMEM_MOST),
    )(*w, gains, tokens, segments)


def order_scatter(classes, late, pieces, begin, rate=46e3, hop=2.5):
    free, events, queue = {}, [], []
    for k in range(len(classes)):
        queue.append((begin if k in late else 0.0, k, 0, 0))
    queue += [(t, -1, n, 0) for n, t in enumerate(pieces)]
    while queue:
        queue.sort()
        ready, k, ph, st = queue.pop(0)
        if k < 0:
            events.append((ph,))
            continue
        i0, i1, order = classes[k]
        events.append((k, ph, st))
        if ph == len(order):
            continue
        dim, done = order[2 - ph], order[: 2 - ph]
        size = size_of(done, i1 - i0)
        if dim == "z":
            ways, moved, waited, follow = ("z+",), size, size, (k, ph + 1, 0)
        elif st == 0:
            ways, moved, waited, follow = (dim + "+", dim + "-"), size, size / 2, (k, ph, 1)
        else:
            ways, moved, waited, follow = (dim + "+", dim + "-"), size / 2, size / 2, (k, ph + 1, 0)
        end = 0.0
        for way in ways:
            first = max(ready, free.get(way, 0.0))
            free[way] = first + moved / rate
            end = max(end, first + waited / rate)
        queue.append((end + hop, *follow))
    return events


def recv_shape(done, n, rows):
    return (*((4,) if "y" in done else ()), n, *((2,) if "z" in done else ()), *((4,) if "x" in done else ()), rows, 128)


def scatter_shapes():
    shapes = []
    for i0, i1, order in CLASSES:
        for ph in range(3):
            dim, done = order[2 - ph], order[: 2 - ph]
            for side in (None,) if dim == "z" else (0, 1):
                (lo, hi), rows = side_of(i0, i1, side)
                one = recv_shape(done, hi - lo, rows[1] - rows[0])
                shapes.append(one if side is None else (3, *one))
    return shapes


def combine(target, refs):
    shape = target.shape[:-2]

    @pl.loop(0, math.prod(shape))
    def _(n):
        index, rest = [], n
        for size in reversed(shape):
            index.insert(0, lax.rem(rest, size))
            rest = rest // size
        value = refs[0][tuple(index)].astype(f32)
        for ref in refs[1:]:
            value = value + ref[tuple(index)].astype(f32)
        target[tuple(index)] = value.astype(bf16)


def add_into(target, refs):
    combine(target, [target, *refs])


def rope_back(grad, cos, sin):
    return grad * cos - half_turn(grad * sin)


def scatter_kernel(
    ffn, buf, other, attn_in, q_raw, k_raw, value, q_rot, k_rot, soft, context, attn_raw, residual,
    d_part, cot, tok, gain_d, gain_h, gpp, cos, sin,
    got, kv_out, gains_out, tok_out,
    acc, pair, own32, send, gacc, grecv, ggot, kv, kvr, gfin, gfinal, gother,
    w, ag, dfull, dctx, dq, dk, dv, part, pstage, pland, gsmall, gheads, land_c, zstage, zland, *rest,
):
    lands = rest[:-10]
    s_sem, r_sem, a_send, a_recv, g_send, g_recv, e_sem, l_sem, f_sem, w_sem = rest[-10:]
    at = coords()
    group = group_peers(at)
    partner = device(at, c=1 - at["c"])
    mirror = device(at, t=1 - at["t"])
    ring = [device(at, x=ahead(at, "x", 1)), device(at, x=ahead(at, "x", -1)), device(at, z=1 - at["z"])]
    ring.append(device(at, x=ahead(at, "x", 2)))
    loads = {}
    for k, (i0, i1, order) in enumerate(CLASSES):
        loads[k] = []
        for y in range(4):
            if y == 3 or k not in ATTN_CLASSES:
                b = 30 + i0 if y == 3 else 10 * y + i0 - 2
                loads[k].append(pltpu.make_async_copy(ffn.at[b : b + i1 - i0], acc.at[y, i0:i1], f_sem.at[k, y]))
    for k in (*range(2, len(CLASSES)), 0, 1):
        for copy in loads[k]:
            copy.start()
    near = pl.ds(pl.multiple_of(at["t"] * 128, 128), 128)
    far = pl.ds(pl.multiple_of((1 - at["t"]) * 128, 128), 128)
    base = at["c"] * 6
    wloads = []
    for y in range(3):
        wloads.append(pltpu.make_async_copy(buf.at[y, 0:2], w.at[pl.ds(base + 2 * y, 2)], w_sem.at[y]))
        wloads.append(pltpu.make_async_copy(other.at[y], w.at[pl.ds(6 - base + 2 * y, 2)], w_sem.at[3 + y]))
    for copy in wloads:
        copy.start()
    enter([device(p) for p in group] + ring + [mirror])
    pending = []

    def push(src, dst, send_sem, recv_sem, to):
        copy = remote(src, dst, send_sem, recv_sem, to)
        copy.start()
        pending.append(copy)

    def await_ref(ref, sem):
        remote(ref, ref, s_sem.at[0, 0, 0], sem, partner).wait_recv()

    zo = device(at, z=1 - at["z"])

    def quarter(c, t, n=1):
        return pl.ds(pl.multiple_of((c * 2 + t) * 128, 128), 128 * n)

    over = remote(d_part.at[quarter(1 - at["c"], 0, 2), :], land_c, e_sem.at[10], e_sem.at[11], partner)
    cross = remote(zstage, zland, e_sem.at[12], e_sem.at[13], mirror)
    over.start()

    def reduce_start():
        over.wait()
        zstage[...] = (d_part[quarter(at["c"], 1 - at["t"]), :] + land_c[far, :]).astype(bf16)
        cross.start()

    def reduce_end():
        cross.wait()
        d_ffn = d_part[quarter(at["c"], at["t"]), :] + land_c[near, :] + zland[...].astype(f32)
        back, gsmall[2:3, :] = norm_back(residual[...], gain_d[2:3, :], d_ffn)
        d_res = cot[...].astype(f32) + back
        tok_out[...] = d_res
        back, gsmall[1:2, :] = norm_back(attn_raw[...], gain_d[1:2, :], d_res)
        dfull[near, :] = back.astype(bf16)
        gsmall[3:4, :] = gpp[...]
        push(dfull.at[near, :], dfull.at[near, :], e_sem.at[6], e_sem.at[7], mirror)

    swap = remote(ag.at[pl.ds(6 - base, 6)], pair, e_sem.at[0], e_sem.at[1], partner)
    pair_copy = remote(pstage, pland, e_sem.at[8], e_sem.at[9], mirror)

    def to_blocks(grad, first):
        grad = grad.astype(bf16)
        for n in range(grad.shape[1] // 128):
            ag[first + n] = grad[:, 128 * n : 128 * n + 128].reshape(2, 4, ROWS, 128)

    def contexts():
        await_ref(dfull.at[far, :], e_sem.at[7])
        for copy in wloads:
            copy.wait()
        dctx[...] = jnp.dot(dfull[...], blocks_of(w, 8, 4), preferred_element_type=f32).astype(bf16)

    def heads():
        dk_rot = jnp.zeros((256, 256), f32)
        d_value = jnp.zeros((256, 256), f32)
        gq = jnp.zeros((1, 256), f32)
        for h in range(2):
            lanes = slice(256 * h, 256 * h + 256)
            d_prob = last_dot(dctx[:, lanes], value[...])
            full = soft[h]
            delta = jnp.sum(full * d_prob, axis=-1, keepdims=True)
            d_score = full * (d_prob - delta) * (256.0 ** -0.5)
            score_b = d_score.astype(bf16)
            dq_norm = rope_back(jnp.dot(score_b, k_rot[...], preferred_element_type=f32), cos[...], sin[...])
            back, gain_part = norm_back(q_raw[:, lanes], gain_h[0:1, :], dq_norm)
            dq[:, lanes] = back.astype(bf16)
            gq = gq + gain_part
            dk_rot = dk_rot + jnp.dot(score_b.T, q_rot[:, lanes], preferred_element_type=f32)
            d_value = d_value + jnp.dot(full.astype(bf16).T, dctx[:, lanes], preferred_element_type=f32)
        back, gk = norm_back(k_raw[...], gain_h[1:2, :], rope_back(dk_rot, cos[...], sin[...]))
        dk[...] = back.astype(bf16)
        dv[...] = d_value.astype(bf16)
        gheads[0:1, :] = gq
        gheads[1:2, :] = gk

    def inputs():
        part[...] = (
            last_dot(dq[...], blocks_of(w, 0, 4))
            + last_dot(dk[...], blocks_of(w, 4, 2))
            + last_dot(dv[...], blocks_of(w, 6, 2))
        )
        pstage[...] = part[far, :].astype(bf16)
        pair_copy.start()

    def weight_grads():
        left = attn_in[...].T
        to_blocks(jnp.dot(left, dq[...], preferred_element_type=f32), 0)
        to_blocks(jnp.dot(left, dk[...], preferred_element_type=f32), 4)
        to_blocks(jnp.dot(left, dv[...], preferred_element_type=f32), 6)

    def out_grads():
        to_blocks(jnp.dot(dfull[...].T, context[...], preferred_element_type=f32), 8)
        swap.start()

    def finish():
        pair_copy.wait()
        d_in = part[near, :] + pland[...].astype(f32)
        back, gsmall[0:1, :] = norm_back(tok[...].astype(f32), gain_d[0:1, :], d_in)
        tok_out[...] = tok_out[...] + back
        folded = fold_gains([gsmall[n : n + 1, :] for n in range(4)], [gheads[n : n + 1, :] for n in range(2)])
        gacc[...] = folded.reshape(2, 4, 8, 128)
        push(gacc.at[1 - at["z"]], grecv.at[0:4], g_send.at[8], g_recv.at[8], zo)

    def merge():
        swap.wait()
        for y in range(3):
            combine(acc.at[y, 0:2], [ag.at[pl.ds(base + 2 * y, 2)], pair.at[2 * y : 2 * y + 2]])

    def small_x():
        await_ref(grecv.at[0:4], g_recv.at[8])
        gacc[at["z"]] = gacc[at["z"]] + grecv[0:4]
        for n in range(1, 4):
            xx = ahead(at, "x", n)
            push(gacc.at[at["z"], xx], grecv.at[4 + n], g_send.at[8 + n], g_recv.at[8 + n], device(at, x=xx))

    pieces = [reduce_start, reduce_end, contexts, heads, weight_grads, out_grads, inputs, merge, finish, small_x]
    times = (3.0, 13.0, 25.0, 28.0, 32.0, 35.0, 37.0, 40.0, 50.0, 54.0)
    slots, position = {}, 0
    for k, (i0, i1, order) in enumerate(CLASSES):
        for ph in range(3):
            count = 1 if order[2 - ph] == "z" else 2
            slots[k, ph] = lands[position : position + count]
            position += count

    for event in order_scatter(CLASSES, ATTN_CLASSES, times, 40.1):
        if len(event) == 1:
            pieces[event[0]]()
            continue
        k, ph, st = event
        i0, i1, order = CLASSES[k]
        if st == 0 and ph == 0:
            for copy in loads[k]:
                copy.wait()
        if st == 0 and ph > 0:
            dim, done = order[3 - ph], order[: 3 - ph]
            if dim == "z":
                (land,) = slots[k, ph - 1]
                await_ref(land, r_sem.at[k, ph - 1, 0])
                add_into(part_of(acc, at, done, "z", at["z"], i0, i1), [land])
            else:
                for side, land in enumerate(slots[k, ph - 1]):
                    await_ref(land.at[1], r_sem.at[k, ph - 1, 3 * side + 1])
                    await_ref(land.at[2], r_sem.at[k, ph - 1, 3 * side + 2])
                    add_into(part_of(acc, at, done, dim, at[dim], i0, i1, side), [land.at[1], land.at[2]])
        if ph == 3:
            continue
        dim, done = order[2 - ph], order[: 2 - ph]
        if dim == "z":
            (land,) = slots[k, ph]
            push(part_of(acc, at, done, "z", 1 - at["z"], i0, i1), land, s_sem.at[k, ph, 0], r_sem.at[k, ph, 0], zo)
            continue
        right, left = device(at, **{dim: ahead(at, dim, 1)}), device(at, **{dim: ahead(at, dim, -1)})
        low, high = slots[k, ph]
        p1, m1, p2 = ahead(at, dim, 1), ahead(at, dim, -1), ahead(at, dim, 2)

        def move(index, side, n, to):
            src = part_of(acc, at, done, dim, index, i0, i1, side)
            push(src, slots[k, ph][side].at[n], s_sem.at[k, ph, 3 * side + n], r_sem.at[k, ph, 3 * side + n], to)

        if st == 0:
            move(p2, 0, 0, right)
            move(p2, 1, 0, left)
            move(p1, 1, 1, right)
            move(m1, 0, 2, left)
        else:
            await_ref(low.at[0], r_sem.at[k, ph, 0])
            add_into(part_of(acc, at, done, dim, p1, i0, i1, 0), [low.at[0]])
            move(p1, 0, 1, right)
            await_ref(high.at[0], r_sem.at[k, ph, 3])
            add_into(part_of(acc, at, done, dim, m1, i0, i1, 1), [high.at[0]])
            move(m1, 1, 2, left)

    mine = at["y"] * 2 + at["c"]
    me = slot_of(at)

    @pl.loop(0, 12)
    def _(i):
        own32[...] = acc[at["y"], i, at["z"], at["x"]].astype(f32)
        for s in range(8):
            send[s, i] = own32[SHARD * s : SHARD * (s + 1), :].astype(bf16)

    for n, p in enumerate(group):
        s = p["y"] * 2 + p["c"]
        push(send.at[s], got.at[me], a_send.at[n], a_recv.at[me], device(p))
    here = pltpu.make_async_copy(send.at[mine], got.at[me], l_sem.at[0])
    here.start()
    gsum = gacc[at["z"], at["x"]]
    for n in range(1, 4):
        await_ref(grecv.at[4 + n], g_recv.at[8 + n])
        gsum = gsum + grecv[4 + n]
    gfin[...] = gsum
    for n, p in enumerate(group):
        push(gfin, ggot.at[mine], g_send.at[n], g_recv.at[mine], device(p))
    here.wait()
    for p in group:
        ref = got.at[slot_of(p)]
        await_ref(ref, a_recv.at[slot_of(p)])
    ggot[mine] = gsum
    for p in group:
        s = p["y"] * 2 + p["c"]
        await_ref(ggot.at[s], g_recv.at[s])
    total = ggot[0]
    for s in range(1, 8):
        total = total + ggot[s]
    gfinal[...] = total
    for k, blocks in enumerate(block_sources()):
        for pos, source in enumerate(blocks):
            if source is not None and source[0] in "kv":
                y, i = divmod(pos, 12)
                j = source[1] + (2 if source[0] == "v" else 0)
                kv[:, j * 128 : (j + 1) * 128] = got[k * 4 + y, i].astype(f32)
    push(kv, kvr, e_sem.at[2], e_sem.at[3], mirror)
    push(gfinal, gother, e_sem.at[4], e_sem.at[5], mirror)
    await_ref(kvr, e_sem.at[3])
    await_ref(gother, e_sem.at[5])
    kv_out[...] = kv[...] + kvr[...]
    gains_out[...] = gfinal[...] + gother[...]
    for copy in pending:
        copy.wait_send()


def result_kernel(got, kv, gains, tok, res, q_out, k_out, v_out, o_out, g_out, u_out, d_out, tok_out, out, *gain_outs):
    outs = {"q": q_out, "o": o_out, "g": g_out, "u": u_out, "d": d_out}
    for k, blocks in enumerate(block_sources()):
        for pos, source in enumerate(blocks):
            if source is not None and source[0] not in "kv":
                y, i = divmod(pos, 12)
                name, j = source
                outs[name][:, j * 128 : (j + 1) * 128] = got[k * 4 + y, i].astype(f32)
    k_out[...] = kv[:, 0:256]
    v_out[...] = kv[:, 256:512]
    tok_out[...] = tok[...]
    out[...] = res[...]
    row = lax.broadcasted_iota(jnp.int32, (8, 128), 0)
    line = jnp.sum(jnp.where(row == lax.rem(lax.axis_index("dp"), 8), gains[...], 0.0), axis=0, keepdims=True)
    for n, ref in enumerate(gain_outs):
        size = ref.shape[1]
        lo = SHARD * n if n < 4 else 4 * SHARD + 4 * (n - 4)
        ref[...] = line[:, lo : lo + size]


def results(got, kv, gains, tok, res):
    widths = (512, 256, 256, 512, 3456, 3456, 3456)
    out = [jax.ShapeDtypeStruct((SHARD, w), f32) for w in widths]
    out += [jax.ShapeDtypeStruct(tok.shape, f32), jax.ShapeDtypeStruct(res.shape, bf16)]
    out += [jax.ShapeDtypeStruct((1, n), f32) for n in (SHARD, SHARD, SHARD, SHARD, 4, 4)]
    return pl.pallas_call(
        result_kernel,
        name="assemble",
        out_shape=tuple(out),
        in_specs=[VMEM_SPEC] * 5,
        out_specs=[VMEM_SPEC] * len(out),
    )(got, kv, gains, tok, res)


def scatter_all(*operands):
    n = len(CLASSES)
    dma = pltpu.SemaphoreType.DMA
    out = [jax.ShapeDtypeStruct((8, 12, SHARD, 128), bf16), jax.ShapeDtypeStruct((SHARD, 512), f32)]
    out += [jax.ShapeDtypeStruct((8, 128), f32), jax.ShapeDtypeStruct((128, 8 * ROWS), f32)]
    return pl.pallas_call(
        scatter_kernel,
        name="attend_back_and_scatter",
        out_shape=tuple(out),
        in_specs=[ANY_SPEC] * 3 + [VMEM_SPEC] * 18,
        out_specs=[VMEM_SPEC] * 4,
        scratch_shapes=[
            pltpu.VMEM((4, 12, 2, 4, ROWS, 128), bf16),
            pltpu.VMEM((6, 2, 4, ROWS, 128), bf16),
            pltpu.VMEM((ROWS, 128), f32),
            pltpu.VMEM((8, 12, SHARD, 128), bf16),
            pltpu.VMEM((2, 4, 8, 128), f32),
            pltpu.VMEM((8, 8, 128), f32),
            pltpu.VMEM((8, 8, 128), f32),
            pltpu.VMEM((SHARD, 512), f32),
            pltpu.VMEM((SHARD, 512), f32),
            pltpu.VMEM((8, 128), f32),
            pltpu.VMEM((8, 128), f32),
            pltpu.VMEM((8, 128), f32),
            pltpu.VMEM((12, 2, 4, ROWS, 128), bf16),
            pltpu.VMEM((12, 2, 4, ROWS, 128), bf16),
            pltpu.VMEM((256, 8 * ROWS), bf16),
            pltpu.VMEM((256, 512), bf16),
            pltpu.VMEM((256, 512), bf16),
            pltpu.VMEM((256, 256), bf16),
            pltpu.VMEM((256, 256), bf16),
            pltpu.VMEM((256, 8 * ROWS), f32),
            pltpu.VMEM((128, 8 * ROWS), bf16),
            pltpu.VMEM((128, 8 * ROWS), bf16),
            pltpu.VMEM((4, 8 * ROWS), f32),
            pltpu.VMEM((2, 256), f32),
            pltpu.VMEM((256, 8 * ROWS), f32),
            pltpu.VMEM((128, 8 * ROWS), bf16),
            pltpu.VMEM((128, 8 * ROWS), bf16),
            *[pltpu.VMEM(s, bf16) for s in scatter_shapes()],
            dma((n, 3, 6)),
            dma((n, 3, 6)),
            dma((8,)),
            dma((8,)),
            dma((12,)),
            dma((12,)),
            dma((14,)),
            dma((6,)),
            dma((n, 4)),
            dma((6,)),
        ],
        compiler_params=pltpu.CompilerParams(collective_id=2, has_side_effects=True, vmem_limit_bytes=VMEM_MOST),
    )(*operands)


def ffn_kernel(
    xs, res, cot, gain, buf,
    out, part, gpp, grads,
    w, dw, ds, xt, dt, gates, ups, land_a, zstage, zland_a,
    w_sem, dw_sem, s_sem, r_sem,
):
    at = coords()
    mirror = device(at, t=1 - at["t"])
    partner = device(at, c=1 - at["c"])
    pairs = 7
    loads = []
    for j in range(pairs):
        for n in range(3):
            lo = n * 14 + 2 * j
            copy = pltpu.make_async_copy(buf.at[place(lo) : place(lo) + 2], w.at[lo : lo + 2], w_sem.at[j, n])
            copy.start()

    def rows(c, t, n=1):
        return pl.ds(pl.multiple_of((c * 2 + t) * 128, 128), 128 * n)

    c, t = at["c"], at["t"]

    def gather(e, full):
        view = lambda cc, tt: full.at[rows(cc, tt), :]
        a = remote(view(c, t), view(c, t), s_sem.at[e, 0], r_sem.at[e, 0], mirror)
        b = remote(view(c, t), view(c, t), s_sem.at[e, 1], r_sem.at[e, 1], partner)
        a.start()
        b.start()
        ref = view(c, 1 - t)
        remote(ref, ref, s_sem.at[e, 0], r_sem.at[e, 0], mirror).wait_recv()
        f = remote(ref, ref, s_sem.at[e, 2], r_sem.at[e, 2], partner)
        f.start()
        one, two = view(1 - c, t), view(1 - c, 1 - t)
        remote(one, one, s_sem.at[e, 0], r_sem.at[e, 1], mirror).wait_recv()
        remote(two, two, s_sem.at[e, 0], r_sem.at[e, 2], mirror).wait_recv()
        for copy in (a, b, f):
            copy.wait_send()

    def reduce(e, land, zland):
        a = remote(part.at[rows(1 - c, 0, 2), :], land, s_sem.at[e, 0], r_sem.at[e, 0], partner)
        a.start()
        a.wait()
        far = pl.ds(pl.multiple_of((1 - t) * 128, 128), 128)
        near = pl.ds(pl.multiple_of(t * 128, 128), 128)
        zstage[...] = (part[rows(c, 1 - t), :] + land[far, :]).astype(bf16)
        b = remote(zstage, zland, s_sem.at[e, 1], r_sem.at[e, 1], mirror)
        b.start()
        kept = part[rows(c, t), :] + land[near, :]
        b.wait()
        return kept + zland[...].astype(f32)

    part[...] = jnp.zeros_like(part)

    def weights(j, n):
        return jnp.concatenate([w[n * 14 + 2 * j], w[n * 14 + 2 * j + 1]], axis=1)

    def rows_dot(a, b):
        return lax.dot_general(a, b, (((1,), (1,)), ((), ())), preferred_element_type=f32)

    @pl.loop(0, pairs)
    def _(j):
        lanes = pl.ds(pl.multiple_of(j * 256, 256), 256)
        for n in range(3):
            pltpu.make_async_copy(buf.at[0:2], w.at[0:2], w_sem.at[j, n]).wait()
        gate = jnp.dot(xs[...], weights(j, 0), preferred_element_type=f32)
        up = jnp.dot(xs[...], weights(j, 1), preferred_element_type=f32)
        gates[:, lanes] = gate
        ups[:, lanes] = up
        act = 0.5 * gate * (1.0 + jnp.tanh(gelu_scale * (gate + gelu_cube * gate * gate * gate)))
        hidden = (act * up).astype(bf16)
        part[...] += rows_dot(hidden, weights(j, 2))

    enter([mirror, partner])
    raw = reduce(1, land_a, zland_a)
    width = raw.shape[1]
    inverse = lax.rsqrt(jnp.sum(raw * raw, axis=-1, keepdims=True) * (1.0 / width) + eps)
    gained = 1.0 + gain[...]
    out[...] = (res[...] + raw * inverse * gained).astype(bf16)
    g = cot[...].astype(f32)
    scaled = g * gained
    mean = jnp.sum(scaled * raw, axis=-1, keepdims=True) * (1.0 / width)
    ds[rows(c, t), :] = (inverse * scaled - raw * inverse * inverse * inverse * mean).astype(bf16)
    gpp[...] = jnp.sum(g * raw * inverse, axis=0, keepdims=True)
    gather(2, ds)
    xt[...] = xs[...].T
    dt[...] = ds[...].T
    part[...] = jnp.zeros_like(part)

    @pl.loop(0, pairs)
    def _(j):
        lanes = pl.ds(pl.multiple_of(j * 256, 256), 256)
        gate, up = gates[:, lanes], ups[:, lanes]
        d_hidden = jnp.dot(ds[...], weights(j, 2), preferred_element_type=f32)
        tanh = jnp.tanh(gelu_scale * (gate + gelu_cube * gate * gate * gate))
        act = 0.5 * gate * (1.0 + tanh)
        slope = 0.5 * (1.0 + tanh) + 0.5 * gate * (1.0 - tanh * tanh) * gelu_scale * (
            1.0 + 3.0 * gelu_cube * gate * gate
        )
        hidden = (act * up).astype(bf16)
        d_gate = (d_hidden * up * slope).astype(bf16)
        d_up = (d_hidden * act).astype(bf16)
        part[...] += rows_dot(d_gate, weights(j, 0)) + rows_dot(d_up, weights(j, 1))
        for n, (left, right) in enumerate(((xt, d_gate), (xt, d_up), (dt, hidden))):
            grad = jnp.dot(left[...], right, preferred_element_type=f32).astype(bf16)
            lo = n * 14 + 2 * j
            dw[lo] = grad[:, :128]
            dw[lo + 1] = grad[:, 128:]
            pltpu.make_async_copy(dw.at[pl.ds(lo, 2)], grads.at[pl.ds(lo, 2)], dw_sem.at[j, n]).start()

    for j in range(pairs):
        for n in range(3):
            lo = n * 14 + 2 * j
            pltpu.make_async_copy(dw.at[lo : lo + 2], grads.at[lo : lo + 2], dw_sem.at[j, n]).wait()


def ffn_all(xs, res, cot, gain, buf):
    dma = pltpu.SemaphoreType.DMA
    tokens, width = res.shape
    return pl.pallas_call(
        ffn_kernel,
        name="ffn_layer",
        out_shape=(
            jax.ShapeDtypeStruct((tokens, width), bf16),
            jax.ShapeDtypeStruct((4 * tokens, width), f32),
            jax.ShapeDtypeStruct((1, width), f32),
            jax.ShapeDtypeStruct((42, width, 128), bf16),
        ),
        in_specs=[VMEM_SPEC] * 4 + [ANY_SPEC],
        out_specs=[VMEM_SPEC] * 3 + [ANY_SPEC],
        scratch_shapes=[
            pltpu.VMEM((42, width, 128), bf16),
            pltpu.VMEM((42, width, 128), bf16),
            pltpu.VMEM((512, width), bf16),
            pltpu.VMEM((width, 512), bf16),
            pltpu.VMEM((width, 512), bf16),
            pltpu.VMEM((512, 1792), f32),
            pltpu.VMEM((512, 1792), f32),
            pltpu.VMEM((256, width), f32),
            pltpu.VMEM((128, width), bf16),
            pltpu.VMEM((128, width), bf16),
            dma((7, 3)),
            dma((7, 3)),
            dma((4, 3)),
            dma((4, 3)),
        ],
        compiler_params=pltpu.CompilerParams(collective_id=3, has_side_effects=True, vmem_limit_bytes=VMEM_MOST),
    )(xs, res, cot, gain, buf)


def local(
    tokens,
    segment_ids,
    w_query,
    w_key,
    w_value,
    w_out,
    gain_query,
    gain_key,
    gain_pre_attn,
    gain_post_attn,
    w_gate,
    w_up,
    w_down,
    gain_pre_ffn,
    gain_post_ffn,
    cotangent,
):
    gains = (gain_pre_attn, gain_post_attn, gain_pre_ffn, gain_post_ffn, gain_query, gain_key)
    packed, lane = 0.0, 0
    for gain in gains:
        packed = packed + jnp.pad(gain.astype(f32), (lane, 128 - lane - gain.shape[0]))
        lane += gain.shape[0]
    packed = jnp.broadcast_to(packed[None], (8, 128))
    width = tokens.shape[1]
    (
        buf, other, attn_in, q_raw, k_raw, value, q_rot, k_rot, soft, context, attn_raw, residual, ffn_full,
        gain_d, gain_h, cos, sin,
    ) = gather_all((w_query, w_key, w_value, w_out, w_gate, w_up, w_down), packed, tokens, segment_ids)
    output, d_part, gpp, ffn_grads = ffn_all(ffn_full, residual, cotangent, gain_d[3:4], buf.reshape(48, width, 128))
    sums = scatter_all(
        ffn_grads.reshape(42, 2, 4, ROWS, 128), buf, other, attn_in, q_raw, k_raw, value, q_rot, k_rot, soft, context,
        attn_raw, residual, d_part, cotangent, tokens, gain_d, gain_h, gpp, cos, sin,
    )
    sums = results(*sums, output)
    s_query, s_key, s_value, s_out, s_gate, s_up, s_down, grad_tokens, output = sums[:9]
    s_pa, s_po, s_pf, s_pp, s_gq, s_gk = [g.reshape(-1) for g in sums[9:]]
    return (
        output, grad_tokens, s_query, s_key, s_value, s_out, s_gq, s_gk,
        s_pa, s_po, s_gate, s_up, s_down, s_pf, s_pp,
    )


def solution(mesh):
    return jax.shard_map(
        local,
        mesh=mesh,
        in_specs=(
            P(("dp", "tensor"), None),
            P("dp", None),
            P("dp", "tensor"),
            P("dp", None),
            P("dp", None),
            P("dp", "tensor"),
            P("dp"),
            P("dp"),
            P("dp"),
            P("dp"),
            P("dp", "tensor"),
            P("dp", "tensor"),
            P("dp", "tensor"),
            P("dp"),
            P("dp"),
            P(("dp", "tensor"), None),
        ),
        out_specs=(
            P(("dp", "tensor"), None),
            P(("dp", "tensor"), None),
            P("dp", "tensor"),
            P("dp", None),
            P("dp", None),
            P("dp", "tensor"),
            P("dp"),
            P("dp"),
            P("dp"),
            P("dp"),
            P("dp", "tensor"),
            P("dp", "tensor"),
            P("dp", "tensor"),
            P("dp"),
            P("dp"),
        ),
        check_vma=False,
    )
```
